32 devices in a mesh: groups: 2 (over x), row: 16 (over z, y, core).
Axes of the slice: x: 2, y: 2, z: 4, core: 2. Of those that a mesh axis runs over, the one named last changes fastest.
Arguments:
- gated_hidden_rows: bfloat16 [2, 384, 28672], P(None, 'groups', 'row'), parts along dimension 1, may hold values from -6 to 6
- down_base_weight: bfloat16 [8192, 28672], P('row'), may hold values from -0.03125 to 0.03125
- adapter_input_factor: bfloat16 [8, 64, 28672], P(None, None, 'row'), may hold values from -0.03125 to 0.03125
- adapter_output_weight: bfloat16 [8, 64, 8192], P(None, None, 'row'), may hold values from -0.75 to 0.75
- request_adapter_index: int32 [2, 384], P(None, 'groups'), parts along dimension 1, may hold values from 0 to 7, as said below
Outputs:
- ffn_out: bfloat16 [2, 384, 8192], P(None, 'groups', 'row'), parts along dimension 1
The draws below stay inside these ranges and needn't reach their ends.
There are 2 independent parts, one for each index of `groups`. The reference program is written for one: setup_inputs(seed, part) draws one part's arguments, and reference() takes and returns one part's arrays. A program takes and returns all parts, laid end to end along the dimension named above; an argument that names none is the same for every part. Nothing has to cross between parts.
Inputs may be any that keep to these rules, and one draw needn't show every extreme that they name: `request_adapter_index`: each entry names one of the 8 adapters; adapter 0 is the resident adapter that is merged into the weights.
All inputs are finite; a program needn't handle non-finite values.
Results may differ from the reference program's by a relative error of at most 0.0038.
Values may be sent and summed in bfloat16 or wider, within the bound.
No kernel may reach another device: no remote copies, remote signals or barrier semaphores. Data moves between devices by JAX's collectives and lax.ppermute only.
A program may use at most 128 MiB of HBM per device.

```python
import jax
import jax.numpy as jnp
from jax import lax

MODEL_WIDTH = 8192
HIDDEN_UNITS = 28672
ADAPTER_RANK = 64
ADAPTER_COUNT = 8
ROWS = 192
STEPS = 2


def draw_request_adapter_index(key, part):
    picks = jax.random.randint(key, (STEPS, ROWS), 0, 2 * ADAPTER_COUNT - 2)
    return jnp.where(picks < ADAPTER_COUNT - 1, picks + 1, 0).astype(jnp.int32)


def block_scale(key, dims, split, smallest, top_value):
    factor_of, own = 1.0, jax.random.fold_in(key, 6)
    for axis_at, blocks in split:
        draws = jnp.exp(jax.random.uniform(jax.random.fold_in(own, axis_at), (blocks,), jnp.float32, smallest / len(split), top_value / len(split)))
        factor_of = factor_of * jnp.repeat(draws, dims[axis_at] // blocks).reshape([-1 if axis == axis_at else 1 for axis in range(len(dims))])
    return factor_of


def gaussian(own_key, shape, scale, bound, cuts=(), kind=jnp.bfloat16):
    drawn = jax.random.normal(own_key, shape, jnp.float32) * scale
    if len(cuts) > 0:
        drawn = block_scale(own_key, shape, cuts, -0.22, 0.18) * drawn
    return jnp.clip(drawn, min=-bound, max=bound).astype(kind)


def setup_inputs(seed: int = 0, part: int = 0) -> dict:
    splits = jax.random.split(jax.random.key(seed), 6)
    own_keys = jax.random.split(jax.random.fold_in(splits[5], part), 6)
    gated_hidden_rows = gaussian(own_keys[0], (STEPS, ROWS, HIDDEN_UNITS), 1.0, 6.0, ((2, 16),))
    down_base_weight = gaussian(splits[1], (MODEL_WIDTH, HIDDEN_UNITS), HIDDEN_UNITS ** -0.5, 0.03125, ((0, 16),))
    adapter_input_factor = gaussian(splits[2], (ADAPTER_COUNT, ADAPTER_RANK, HIDDEN_UNITS), HIDDEN_UNITS ** -0.5, 0.03125, ((2, 16),))
    adapter_output_weight = gaussian(splits[3], (ADAPTER_COUNT, ADAPTER_RANK, MODEL_WIDTH), ADAPTER_RANK ** -0.5, 0.75, ((2, 16),))
    request_adapter_index = draw_request_adapter_index(jax.random.fold_in(jax.random.fold_in(splits[5], part), 71), part)
    return dict(gated_hidden_rows=gated_hidden_rows, down_base_weight=down_base_weight, adapter_input_factor=adapter_input_factor, adapter_output_weight=adapter_output_weight, request_adapter_index=request_adapter_index)


def select_pair(project_rows, adapter_labels, request_count, rank_index):
    choose = (adapter_labels[:, None] == jnp.arange(request_count, dtype=jnp.int32)[None, :]).astype(jnp.float32)
    total = project_rows.shape[0]
    own = jnp.sum(project_rows.reshape(total, request_count, rank_index) * choose[:, :, None], axis=1)
    resident_weight = project_rows[:, :rank_index]
    keep = (adapter_labels != 0).astype(jnp.float32)[:, None]
    return jnp.concatenate([own, resident_weight], axis=1) * keep


def expand_factor(shrunk_rows, adapter_labels, adapter_output_weight):
    request_count = adapter_output_weight.shape[0]
    rank_index = adapter_output_weight.shape[1]
    total = shrunk_rows.shape[0]
    choose = (adapter_labels[:, None] == jnp.arange(request_count, dtype=jnp.int32)[None, :]).astype(jnp.float32)
    spread = (choose[:, :, None] * shrunk_rows[:, None, :rank_index].astype(jnp.float32)).reshape(total, request_count * rank_index)
    operand = jnp.concatenate([spread.astype(jnp.bfloat16), shrunk_rows[:, rank_index:]], axis=1)
    stacked_weights = jnp.concatenate([adapter_output_weight.reshape(request_count * rank_index, adapter_output_weight.shape[2]), -adapter_output_weight[0]], axis=0)
    return jnp.dot(operand, stacked_weights, preferred_element_type=jnp.float32)


def reference(gated_hidden_rows, down_base_weight, adapter_input_factor, adapter_output_weight, request_adapter_index):
    merged_weight = down_base_weight.astype(jnp.float32) + jnp.dot(adapter_output_weight[0].T, adapter_input_factor[0], preferred_element_type=jnp.float32)
    flattened_rows = gated_hidden_rows.reshape(STEPS * ROWS, HIDDEN_UNITS)
    adapter_labels = request_adapter_index.reshape(STEPS * ROWS)
    base = jnp.dot(flattened_rows.astype(jnp.float32), merged_weight.T, precision=lax.Precision.HIGHEST)
    project_rows = jnp.dot(flattened_rows, adapter_input_factor.reshape(ADAPTER_COUNT * ADAPTER_RANK, HIDDEN_UNITS).T, preferred_element_type=jnp.float32)
    shrunk_rows = select_pair(project_rows, adapter_labels, ADAPTER_COUNT, ADAPTER_RANK).astype(jnp.bfloat16)
    adapter_update = expand_factor(shrunk_rows, adapter_labels, adapter_output_weight)
    return (base + adapter_update).astype(jnp.bfloat16).reshape(STEPS, ROWS, MODEL_WIDTH)
```

```python
import jax
import jax.numpy as jnp
import numpy as np
from jax import lax
from jax.experimental import pallas as pl
from jax.experimental.pallas import tpu as pltpu
from jax.sharding import PartitionSpec as P


LANES = 128


def chip_ring(mesh):
    line = mesh.devices.reshape(mesh.devices.shape[0], -1)[0]
    chips = {}
    for at, device in enumerate(line):
        place = tuple(getattr(device, "coords", (at, 0, 0)))
        chips.setdefault(place, []).append(at)
    places = list(chips)
    if len({len(c) for c in chips.values()}) != 1:
        return [[at] for at in range(len(line))]
    used = [k for k in range(len(places[0])) if len({p[k] for p in places}) > 1]
    if len(used) == 2:
        sizes = [len({p[k] for p in places}) for k in used]
        if 2 in sizes and sizes[0] * sizes[1] == len(places):
            short = used[sizes.index(2)]
            long = used[0] if short == used[1] else used[1]
            low = min(p[short] for p in places)
            up = sorted((p for p in places if p[short] == low), key=lambda p: p[long])
            down = sorted((p for p in places if p[short] != low), key=lambda p: -p[long])
            places = up + down
    return [chips[p] for p in places]


def labels_onehot(adapter_labels, count):
    return adapter_labels[:, None] == jnp.arange(count, dtype=jnp.int32)[None, :]


def select_both(project_rows, adapter_labels, count, rank):
    choose = labels_onehot(adapter_labels, count).astype(jnp.float32)
    total = project_rows.shape[0]
    own = jnp.sum(project_rows.reshape(total, count, rank) * choose[:, :, None], axis=1)
    return jnp.concatenate([own, project_rows[:, :rank]], axis=1)


def expand_factor(shrunk_rows, adapter_labels, adapter_output_weight):
    count, rank, width = adapter_output_weight.shape
    total = shrunk_rows.shape[0]
    choose = labels_onehot(adapter_labels, count).astype(jnp.float32)
    spread = (choose[:, :, None] * shrunk_rows[:, None, :rank].astype(jnp.float32)).reshape(
        total, count * rank
    )
    operand = jnp.concatenate([spread.astype(jnp.bfloat16), shrunk_rows[:, rank:]], axis=1)
    stacked = jnp.concatenate(
        [adapter_output_weight.reshape(count * rank, width), -adapter_output_weight[0]], axis=0
    )
    return jnp.dot(operand, stacked, preferred_element_type=jnp.float32)


def sum_over_row(summand, axis_size):
    rows, cols = summand.shape
    if rows % axis_size:
        return lax.psum(summand, "row")
    parts = lax.all_to_all(summand, "row", 0, 0, tiled=True)
    mine = jnp.sum(parts.reshape(axis_size, rows // axis_size, cols), axis=0)
    spread = jnp.broadcast_to(mine[None], (axis_size,) + mine.shape).reshape(rows, cols)
    return lax.all_to_all(spread, "row", 0, 0, tiled=True)


def chunk_matmul(chunks, starts, first, weight, before, extra, out_dtype):
    count = len(chunks)
    rows, units = chunks[0].shape
    features = weight.shape[0]
    added = [a for a in (before, extra) if a is not None]

    def body(starts_ref, *refs):
        x_refs = refs[:count]
        w_ref = refs[count]
        add_refs = refs[count + 1 : count + 1 + len(added)]
        out_ref, x_buf, w_buf, x_sem, w_sem = refs[count + 1 + len(added) :]
        copies = []
        for k in range(count):
            start = pl.multiple_of(starts_ref[first + k] * LANES, LANES)
            cx = pltpu.make_async_copy(x_refs[k], x_buf.at[k], x_sem.at[k])
            cw = pltpu.make_async_copy(w_ref.at[:, pl.ds(start, units)], w_buf.at[k], w_sem.at[k])
            cw.start()
            cx.start()
            copies.append((cx, cw))
        total = None
        for k in range(count):
            copies[k][1].wait()
            copies[k][0].wait()
            part = lax.dot_general(
                x_buf[k], w_buf[k], (((1,), (1,)), ((), ())), preferred_element_type=jnp.float32
            )
            total = part if total is None else total + part
        for ref in add_refs:
            total = total + ref[...]
        out_ref[...] = total.astype(out_dtype)

    anywhere = pl.BlockSpec(memory_space=pl.ANY)
    vmem = pl.BlockSpec(memory_space=pltpu.VMEM)
    return pl.pallas_call(
        body,
        out_shape=jax.ShapeDtypeStruct((rows, features), out_dtype),
        in_specs=[pl.BlockSpec(memory_space=pltpu.SMEM)]
        + [anywhere] * (count + 1)
        + [vmem] * len(added),
        out_specs=vmem,
        scratch_shapes=[
            pltpu.VMEM((count, rows, units), jnp.bfloat16),
            pltpu.VMEM((count, features, units), jnp.bfloat16),
            pltpu.SemaphoreType.DMA((count,)),
            pltpu.SemaphoreType.DMA((count,)),
        ],
        cost_estimate=pl.CostEstimate(
            flops=2 * count * rows * units * features,
            transcendentals=0,
            bytes_accessed=2 * count * units * (rows + features) + 8 * rows * features,
        ),
        compiler_params=pltpu.CompilerParams(vmem_limit_bytes=48 << 20),
    )(starts, *chunks, weight, *added)


def solution(mesh):
    axis_size = mesh.shape["row"]
    ring = chip_ring(mesh)
    chips, cores = len(ring), len(ring[0])
    forward = [(ring[p][c], ring[(p + 1) % chips][c]) for p in range(chips) for c in range(cores)]
    backward = [(b, a) for a, b in forward]
    partner = [(members[c], members[1 - c]) for members in ring for c in range(cores)] if cores == 2 else []

    def local(
        gated_hidden_rows,
        down_base_weight,
        adapter_input_factor,
        adapter_output_weight,
        request_adapter_index,
    ):
        steps, requests, device_units = gated_hidden_rows.shape
        count, rank, _ = adapter_input_factor.shape
        features = down_base_weight.shape[0]
        total = steps * requests
        flat = gated_hidden_rows.reshape(total, device_units)
        adapter_labels = request_adapter_index.reshape(total)
        project_rows = jnp.dot(
            flat,
            adapter_input_factor.reshape(count * rank, device_units).T,
            preferred_element_type=jnp.float32,
        )
        summed = sum_over_row(
            select_both(project_rows, adapter_labels, count, rank), axis_size
        )
        keep = (adapter_labels != 0).astype(jnp.float32)[:, None]
        shrunk_rows = (summed * keep).astype(jnp.bfloat16)
        extra = jnp.dot(
            summed[:, rank:],
            adapter_output_weight[0].astype(jnp.float32),
            precision=lax.Precision.HIGHEST,
        ) + expand_factor(shrunk_rows, adapter_labels, adapter_output_weight)

        if cores != 2 or chips < 2 or chips % 2 or device_units % (2 * LANES):
            base = lax.dot_general(
                lax.all_gather(flat, "row", axis=1, tiled=True),
                down_base_weight,
                (((1,), (1,)), ((), ())),
                preferred_element_type=jnp.float32,
            )
            return (base + extra).astype(jnp.bfloat16).reshape(steps, requests, features)

        half = device_units // 2
        where = []

        def start_of(offset, other, part):
            where.append((offset, other, part))
            return len(where) - 1

        own = [flat[:, :half], flat[:, half:]]
        hops = 2 * (chips // 2) - 1
        ups, downs = list(own), list(own)
        found = []
        for part in range(2):
            other = lax.ppermute(own[part], "row", partner)
            found += [(own[part], start_of(0, False, part)), (other, start_of(0, True, part))]
        batches = [found]
        for s in range(hops):
            up_part, down_part, d = s % 2, 1 - s % 2, s // 2 + 1
            ups[up_part] = lax.ppermute(ups[up_part], "row", forward)
            downs[down_part] = lax.ppermute(downs[down_part], "row", backward)
            found = []
            for data, offset, part in (
                (ups[up_part], -d, up_part), (downs[down_part], d, down_part)
            ):
                other = lax.ppermute(data, "row", partner)
                found.append((data, start_of(offset, False, part)))
                found.append((other, start_of(offset, True, part)))
            batches.append(found)
        order = [where[at] for found in batches for _, at in found]
        table = np.zeros((axis_size, len(order)), np.int32)
        for p, members in enumerate(ring):
            for c, at in enumerate(members):
                for k, (offset, other, part) in enumerate(order):
                    source = ring[(p + offset) % chips][1 - c if other else c]
                    table[at, k] = (source * 2 + part) * (half // LANES)
        starts = jnp.asarray(table)[lax.axis_index("row")]
        acc = None
        done = 0
        for k, found in enumerate(batches):
            last = k == len(batches) - 1
            acc = chunk_matmul(
                [data for data, _ in found],
                starts,
                done,
                down_base_weight,
                acc,
                extra if last else None,
                jnp.bfloat16 if last else jnp.float32,
            )
            done += len(found)
        return acc.reshape(steps, requests, features)

    placed = (
        P(None, "groups", "row"),
        P("row", None),
        P(None, None, "row"),
        P(None, None, "row"),
        P(None, "groups"),
    )

    return jax.shard_map(
        local, mesh=mesh, in_specs=placed, out_specs=P(None, "groups", "row"), check_vma=False
    )
```

```python
import jax
import jax.numpy as jnp
import numpy as np
from jax import lax
from jax.experimental import pallas as pl
from jax.experimental.pallas import tpu as pltpu
from jax.sharding import PartitionSpec as P


LANES = 128


def chip_ring(mesh):
    line = mesh.devices.reshape(mesh.devices.shape[0], -1)[0]
    chips = {}
    for at, device in enumerate(line):
        place = tuple(getattr(device, "coords", (at, 0, 0)))
        chips.setdefault(place, []).append(at)
    places = list(chips)
    if len({len(c) for c in chips.values()}) != 1:
        return [[at] for at in range(len(line))]
    used = [k for k in range(len(places[0])) if len({p[k] for p in places}) > 1]
    if len(used) == 2:
        sizes = [len({p[k] for p in places}) for k in used]
        if 2 in sizes and sizes[0] * sizes[1] == len(places):
            short = used[sizes.index(2)]
            long = used[0] if short == used[1] else used[1]
            low = min(p[short] for p in places)
            up = sorted((p for p in places if p[short] == low), key=lambda p: p[long])
            down = sorted((p for p in places if p[short] != low), key=lambda p: -p[long])
            places = up + down
    return [chips[p] for p in places]


def project_selected(rows, labels, factors):
    count, rank, units = factors.shape
    total = rows.shape[0]
    wide = count * rank

    def body(x_ref, l_ref, a_ref, o_ref):
        full = lax.dot_general(
            x_ref[...], a_ref[...], (((1,), (1,)), ((), ())), preferred_element_type=jnp.float32
        )
        own = jnp.zeros((total, rank), jnp.float32)
        for k in range(count):
            own = own + jnp.where(l_ref[...] == k, full[:, k * rank : (k + 1) * rank], 0.0)
        o_ref[...] = jnp.concatenate([own, full[:, :rank]], axis=1)

    vmem = pl.BlockSpec(memory_space=pltpu.VMEM)
    return pl.pallas_call(
        body,
        out_shape=jax.ShapeDtypeStruct((total, 2 * rank), jnp.float32),
        in_specs=[vmem] * 3,
        out_specs=vmem,
        cost_estimate=pl.CostEstimate(
            flops=2 * total * wide * units,
            transcendentals=0,
            bytes_accessed=2 * units * (total + wide) + 8 * total * rank,
        ),
        compiler_params=pltpu.CompilerParams(vmem_limit_bytes=32 << 20),
    )(rows, labels[:, None], factors.reshape(wide, units))


def labels_onehot(adapter_labels, count):
    return adapter_labels[:, None] == jnp.arange(count, dtype=jnp.int32)[None, :]


def expand_factor(shrunk_rows, adapter_labels, adapter_output_weight):
    count, rank, width = adapter_output_weight.shape
    total = shrunk_rows.shape[0]
    choose = labels_onehot(adapter_labels, count).astype(jnp.float32)
    spread = (choose[:, :, None] * shrunk_rows[:, None, :rank].astype(jnp.float32)).reshape(
        total, count * rank
    )
    operand = jnp.concatenate([spread.astype(jnp.bfloat16), shrunk_rows[:, rank:]], axis=1)
    stacked = jnp.concatenate(
        [adapter_output_weight.reshape(count * rank, width), -adapter_output_weight[0]], axis=0
    )
    return jnp.dot(operand, stacked, preferred_element_type=jnp.float32)


def sum_over_row(summand, axis_size):
    rows, cols = summand.shape
    if rows % axis_size:
        return lax.psum(summand, "row")
    parts = lax.all_to_all(summand, "row", 0, 0, tiled=True)
    mine = jnp.sum(parts.reshape(axis_size, rows // axis_size, cols), axis=0)
    spread = jnp.broadcast_to(mine[None], (axis_size,) + mine.shape).reshape(rows, cols)
    return lax.all_to_all(spread, "row", 0, 0, tiled=True)


def chunk_matmul(chunks, starts, first, weight, before, extra, out_dtype):
    count = len(chunks)
    rows, units = chunks[0].shape
    features = weight.shape[0]
    added = [a for a in (before, extra) if a is not None]

    def body(starts_ref, *refs):
        x_refs = refs[:count]
        w_ref = refs[count]
        add_refs = refs[count + 1 : count + 1 + len(added)]
        out_ref, x_buf, w_buf, x_sem, w_sem = refs[count + 1 + len(added) :]
        copies = []
        for k in range(count):
            start = pl.multiple_of(starts_ref[first + k] * LANES, LANES)
            cx = pltpu.make_async_copy(x_refs[k], x_buf.at[k], x_sem.at[k])
            cw = pltpu.make_async_copy(w_ref.at[:, pl.ds(start, units)], w_buf.at[k], w_sem.at[k])
            cw.start()
            cx.start()
            copies.append((cx, cw))
        total = None
        for k in range(count):
            copies[k][1].wait()
            copies[k][0].wait()
            part = lax.dot_general(
                x_buf[k], w_buf[k], (((1,), (1,)), ((), ())), preferred_element_type=jnp.float32
            )
            total = part if total is None else total + part
        for ref in add_refs:
            total = total + ref[...]
        out_ref[...] = total.astype(out_dtype)

    anywhere = pl.BlockSpec(memory_space=pl.ANY)
    vmem = pl.BlockSpec(memory_space=pltpu.VMEM)
    return pl.pallas_call(
        body,
        out_shape=jax.ShapeDtypeStruct((rows, features), out_dtype),
        in_specs=[pl.BlockSpec(memory_space=pltpu.SMEM)]
        + [anywhere] * (count + 1)
        + [vmem] * len(added),
        out_specs=vmem,
        scratch_shapes=[
            pltpu.VMEM((count, rows, units), jnp.bfloat16),
            pltpu.VMEM((count, features, units), jnp.bfloat16),
            pltpu.SemaphoreType.DMA((count,)),
            pltpu.SemaphoreType.DMA((count,)),
        ],
        cost_estimate=pl.CostEstimate(
            flops=2 * count * rows * units * features,
            transcendentals=0,
            bytes_accessed=2 * count * units * (rows + features) + 8 * rows * features,
        ),
        compiler_params=pltpu.CompilerParams(vmem_limit_bytes=48 << 20),
    )(starts, *chunks, weight, *added)


def solution(mesh):
    axis_size = mesh.shape["row"]
    ring = chip_ring(mesh)
    chips, cores = len(ring), len(ring[0])
    forward = [(ring[p][c], ring[(p + 1) % chips][c]) for p in range(chips) for c in range(cores)]
    backward = [(b, a) for a, b in forward]
    partner = [(members[c], members[1 - c]) for members in ring for c in range(cores)] if cores == 2 else []

    def local(
        gated_hidden_rows,
        down_base_weight,
        adapter_input_factor,
        adapter_output_weight,
        request_adapter_index,
    ):
        steps, requests, device_units = gated_hidden_rows.shape
        _, rank, _ = adapter_input_factor.shape
        features = down_base_weight.shape[0]
        total = steps * requests
        flat = gated_hidden_rows.reshape(total, device_units)
        adapter_labels = request_adapter_index.reshape(total)
        summand = project_selected(flat, adapter_labels, adapter_input_factor)
        summed = sum_over_row(summand, axis_size)
        keep = (adapter_labels != 0).astype(jnp.float32)[:, None]
        shrunk_rows = (summed * keep).astype(jnp.bfloat16)
        extra = jnp.dot(
            summed[:, rank:],
            adapter_output_weight[0].astype(jnp.float32),
            precision=lax.Precision.HIGHEST,
        ) + expand_factor(shrunk_rows, adapter_labels, adapter_output_weight)

        if cores != 2 or chips < 2 or chips % 2 or device_units % (2 * LANES):
            base = lax.dot_general(
                lax.all_gather(flat, "row", axis=1, tiled=True),
                down_base_weight,
                (((1,), (1,)), ((), ())),
                preferred_element_type=jnp.float32,
            )
            return (base + extra).astype(jnp.bfloat16).reshape(steps, requests, features)

        half = device_units // 2
        where = []

        def start_of(offset, other, part):
            where.append((offset, other, part))
            return len(where) - 1

        own = [flat[:, :half], flat[:, half:]]
        hops = 2 * (chips // 2) - 1
        ups, downs = list(own), list(own)
        found = []
        for part in range(2):
            other = lax.ppermute(own[part], "row", partner)
            found += [(own[part], start_of(0, False, part)), (other, start_of(0, True, part))]
        batches = [found]
        for s in range(hops):
            up_part, down_part, d = s % 2, 1 - s % 2, s // 2 + 1
            ups[up_part] = lax.ppermute(ups[up_part], "row", forward)
            downs[down_part] = lax.ppermute(downs[down_part], "row", backward)
            found = []
            for data, offset, part in (
                (ups[up_part], -d, up_part), (downs[down_part], d, down_part)
            ):
                other = lax.ppermute(data, "row", partner)
                found.append((data, start_of(offset, False, part)))
                found.append((other, start_of(offset, True, part)))
            if s == hops - 1:
                batches += [found[::2], found[1::2]]
            else:
                batches.append(found)
        order = [where[at] for found in batches for _, at in found]
        table = np.zeros((axis_size, len(order)), np.int32)
        for p, members in enumerate(ring):
            for c, at in enumerate(members):
                for k, (offset, other, part) in enumerate(order):
                    source = ring[(p + offset) % chips][1 - c if other else c]
                    table[at, k] = (source * 2 + part) * (half // LANES)
        starts = jnp.asarray(table)[lax.axis_index("row")]
        acc = None
        done = 0
        for k, found in enumerate(batches):
            last = k == len(batches) - 1
            acc = chunk_matmul(
                [data for data, _ in found],
                starts,
                done,
                down_base_weight,
                acc,
                extra if k == hops - 1 else None,
                jnp.bfloat16 if last else jnp.float32,
            )
            done += len(found)
        return acc.reshape(steps, requests, features)

    placed = (
        P(None, "groups", "row"),
        P("row", None),
        P(None, None, "row"),
        P(None, None, "row"),
        P(None, "groups"),
    )

    return jax.shard_map(
        local, mesh=mesh, in_specs=placed, out_specs=P(None, "groups", "row"), check_vma=False
    )
```

```python
import jax
import jax.numpy as jnp
import numpy as np
from jax import lax
from jax.experimental import pallas as pl
from jax.experimental.pallas import tpu as pltpu
from jax.sharding import PartitionSpec as P


LANES = 128


def chip_ring(mesh):
    line = mesh.devices.reshape(mesh.devices.shape[0], -1)[0]
    chips = {}
    for at, device in enumerate(line):
        place = tuple(getattr(device, "coords", (at, 0, 0)))
        chips.setdefault(place, []).append(at)
    places = list(chips)
    if len({len(c) for c in chips.values()}) != 1:
        return [[at] for at in range(len(line))], False
    used = [k for k in range(len(places[0])) if len({p[k] for p in places}) > 1]
    if len(used) == 2:
        sizes = [len({p[k] for p in places}) for k in used]
        if 2 in sizes and sizes[0] * sizes[1] == len(places):
            short = used[sizes.index(2)]
            long = used[0] if short == used[1] else used[1]
            low = min(p[short] for p in places)
            up = sorted((p for p in places if p[short] == low), key=lambda p: p[long])
            down = sorted((p for p in places if p[short] != low), key=lambda p: -p[long])
            places = up + down
            return [chips[p] for p in places], True
    return [chips[p] for p in places], False


def project_selected(rows, labels, factors, first):
    count, rank, units = factors.shape
    total = rows.shape[0]
    wide = count * rank
    part = total // 2

    def body(f_ref, x_ref, l_ref, a_ref, mine_ref, other_ref, s_ref):
        full = lax.dot_general(
            x_ref[...], a_ref[...], (((1,), (1,)), ((), ())), preferred_element_type=jnp.float32
        )
        own = jnp.zeros((total, rank), jnp.float32)
        for k in range(count):
            own = own + jnp.where(l_ref[...] == k, full[:, k * rank : (k + 1) * rank], 0.0)
        s_ref[...] = jnp.concatenate([own, full[:, :rank]], axis=1)
        at = f_ref[0]
        mine_ref[...] = s_ref[pl.ds(pl.multiple_of(at * part, 8), part), :]
        other_ref[...] = s_ref[pl.ds(pl.multiple_of((1 - at) * part, 8), part), :]

    vmem = pl.BlockSpec(memory_space=pltpu.VMEM)
    shape = jax.ShapeDtypeStruct((part, 2 * rank), jnp.float32)
    return pl.pallas_call(
        body,
        out_shape=(shape, shape),
        in_specs=[pl.BlockSpec(memory_space=pltpu.SMEM)] + [vmem] * 3,
        out_specs=(vmem, vmem),
        scratch_shapes=[pltpu.VMEM((total, 2 * rank), jnp.float32)],
        cost_estimate=pl.CostEstimate(
            flops=2 * total * wide * units,
            transcendentals=0,
            bytes_accessed=2 * units * (total + wide) + 8 * total * rank,
        ),
        compiler_params=pltpu.CompilerParams(vmem_limit_bytes=32 << 20),
    )(first.reshape(1), rows, labels[:, None], factors.reshape(wide, units))


def labels_onehot(adapter_labels, count):
    return adapter_labels[:, None] == jnp.arange(count, dtype=jnp.int32)[None, :]


def select_both(project_rows, adapter_labels, count, rank):
    choose = labels_onehot(adapter_labels, count).astype(jnp.float32)
    total = project_rows.shape[0]
    own = jnp.sum(project_rows.reshape(total, count, rank) * choose[:, :, None], axis=1)
    return jnp.concatenate([own, project_rows[:, :rank]], axis=1)


def expand_factor(shrunk_rows, adapter_labels, adapter_output_weight):
    count, rank, width = adapter_output_weight.shape
    total = shrunk_rows.shape[0]
    choose = labels_onehot(adapter_labels, count).astype(jnp.float32)
    spread = (choose[:, :, None] * shrunk_rows[:, None, :rank].astype(jnp.float32)).reshape(
        total, count * rank
    )
    operand = jnp.concatenate([spread.astype(jnp.bfloat16), shrunk_rows[:, rank:]], axis=1)
    stacked = jnp.concatenate(
        [adapter_output_weight.reshape(count * rank, width), -adapter_output_weight[0]], axis=0
    )
    return jnp.dot(operand, stacked, preferred_element_type=jnp.float32)


def adapter_terms(summed, labels, outputs):
    rank = outputs.shape[1]
    keep = (labels != 0).astype(jnp.float32)[:, None]
    shrunk_rows = (summed * keep).astype(jnp.bfloat16)
    resident = jnp.dot(
        summed[:, rank:], outputs[0].astype(jnp.float32), precision=lax.Precision.HIGHEST
    )
    return resident + expand_factor(shrunk_rows, labels, outputs)


def sum_over_row(summand, axis_size):
    rows, cols = summand.shape
    if rows % axis_size:
        return lax.psum(summand, "row")
    parts = lax.all_to_all(summand, "row", 0, 0, tiled=True)
    mine = jnp.sum(parts.reshape(axis_size, rows // axis_size, cols), axis=0)
    spread = jnp.broadcast_to(mine[None], (axis_size,) + mine.shape).reshape(rows, cols)
    return lax.all_to_all(spread, "row", 0, 0, tiled=True)


def swap(rows, at, pairs):
    part = rows.shape[0] // 2
    low, high = rows[:part], rows[part:]
    got = lax.ppermute(jnp.where(at == 0, high, low), "row", pairs)
    return jnp.where(at == 0, low, high) + got


def join(part, at, pairs):
    got = lax.ppermute(part, "row", pairs)
    return jnp.concatenate([jnp.where(at == 0, part, got), jnp.where(at == 0, got, part)], axis=0)


def sum_by_stages(mine, other, core, side, partner, across, lines):
    got = lax.ppermute(other, "row", partner)
    rows = swap(mine + got, side, across)
    size = len(lines[0])
    piece = rows.shape[0] // size
    parts = lax.all_to_all(rows, "row", 0, 0, axis_index_groups=lines, tiled=True)
    total = jnp.sum(parts.reshape(size, piece, rows.shape[1]), axis=0)
    spread = jnp.broadcast_to(total[None], (size,) + total.shape).reshape(rows.shape)
    whole = lax.all_to_all(spread, "row", 0, 0, axis_index_groups=lines, tiled=True)
    return join(join(whole, side, across), core, partner)


def chunk_matmul(chunks, starts, first, weight, before, extra, out_dtype):
    count = len(chunks)
    rows = chunks[0].shape[0]
    widths = [c.shape[1] for c in chunks]
    features = weight.shape[0]
    added = [a for a in (before, extra) if a is not None]

    def body(starts_ref, *refs):
        x_refs = refs[:count]
        w_ref = refs[count]
        add_refs = refs[count + 1 : count + 1 + len(added)]
        rest = refs[count + 1 + len(added) :]
        out_ref, x_bufs, w_bufs = rest[0], rest[1 : 1 + count], rest[1 + count : 1 + 2 * count]
        x_sem, w_sem = rest[1 + 2 * count :]
        copies = []
        for k in range(count):
            start = pl.multiple_of(starts_ref[first + k] * LANES, LANES)
            cx = pltpu.make_async_copy(x_refs[k], x_bufs[k], x_sem.at[k])
            cw = pltpu.make_async_copy(w_ref.at[:, pl.ds(start, widths[k])], w_bufs[k], w_sem.at[k])
            cw.start()
            cx.start()
            copies.append((cx, cw))
        total = None
        for k in range(count):
            copies[k][1].wait()
            copies[k][0].wait()
            part = lax.dot_general(
                x_bufs[k][...], w_bufs[k][...], (((1,), (1,)), ((), ())), preferred_element_type=jnp.float32
            )
            total = part if total is None else total + part
        for ref in add_refs:
            total = total + ref[...]
        out_ref[...] = total.astype(out_dtype)

    anywhere = pl.BlockSpec(memory_space=pl.ANY)
    vmem = pl.BlockSpec(memory_space=pltpu.VMEM)
    return pl.pallas_call(
        body,
        out_shape=jax.ShapeDtypeStruct((rows, features), out_dtype),
        in_specs=[pl.BlockSpec(memory_space=pltpu.SMEM)]
        + [anywhere] * (count + 1)
        + [vmem] * len(added),
        out_specs=vmem,
        scratch_shapes=[pltpu.VMEM((rows, w), jnp.bfloat16) for w in widths]
        + [pltpu.VMEM((features, w), jnp.bfloat16) for w in widths]
        + [
            pltpu.SemaphoreType.DMA((count,)),
            pltpu.SemaphoreType.DMA((count,)),
        ],
        cost_estimate=pl.CostEstimate(
            flops=2 * rows * sum(widths) * features,
            transcendentals=0,
            bytes_accessed=2 * sum(widths) * (rows + features) + 8 * rows * features,
        ),
        compiler_params=pltpu.CompilerParams(vmem_limit_bytes=48 << 20),
    )(starts, *chunks, weight, *added)


def solution(mesh):
    axis_size = mesh.shape["row"]
    ring, snake = chip_ring(mesh)
    chips, cores = len(ring), len(ring[0])
    forward = [(ring[p][c], ring[(p + 1) % chips][c]) for p in range(chips) for c in range(cores)]
    backward = [(b, a) for a, b in forward]
    partner = [(members[c], members[1 - c]) for members in ring for c in range(cores)] if cores == 2 else []

    long = chips // 2
    across = [(ring[p][c], ring[chips - 1 - p][c]) for p in range(chips) for c in range(cores)]
    lines = [
        [ring[p][c] for p in range(lo, lo + long)] for lo in (0, long) for c in range(cores)
    ]
    place = np.zeros((axis_size, 2), np.int32)
    for p, members in enumerate(ring):
        for c, at in enumerate(members):
            place[at] = c, int(p >= long)

    def plain(flat, weight, factors, outputs, labels):
        count, rank, units = factors.shape
        project_rows = jnp.dot(
            flat, factors.reshape(count * rank, units).T, preferred_element_type=jnp.float32
        )
        summed = sum_over_row(select_both(project_rows, labels, count, rank), axis_size)
        base = lax.dot_general(
            lax.all_gather(flat, "row", axis=1, tiled=True),
            weight,
            (((1,), (1,)), ((), ())),
            preferred_element_type=jnp.float32,
        )
        return (base + adapter_terms(summed, labels, outputs)).astype(jnp.bfloat16)

    def ringed(flat, weight, factors, outputs, labels):
        device_units = flat.shape[1]
        half = device_units // 2
        tiles = half // LANES
        cut = (tiles - tiles * 3 // 7) * LANES
        me = lax.axis_index("row")
        core, side = [jnp.asarray(place)[me][k] for k in range(2)]
        mine, other = project_selected(flat, labels, factors, core)
        summed = sum_by_stages(mine, other, core, side, partner, across, lines)
        extra = adapter_terms(summed, labels, outputs)

        plan = [(s // 2 + 1, s % 2, 0, half) for s in range(2 * long - 2)]
        plan += [(long, 0, 0, cut), (long, 0, cut, half - cut)]
        own = [flat[:, :half], flat[:, half:]]
        beside = lax.ppermute(flat, "row", partner)
        batches = [[(flat, 0, False, 0, 0), (beside, 0, True, 0, 0)]]
        held = {"up": list(own), "down": list(own)}
        for distance, turn, column, width in plan:
            found = []
            for way, pairs, part in (("up", forward, turn), ("down", backward, 1 - turn)):
                send = held[way][part]
                if width < half:
                    send = send[:, column : column + width]
                data = lax.ppermute(send, "row", pairs)
                if width == half:
                    held[way][part] = data
                beside = lax.ppermute(data, "row", partner)
                offset = -distance if way == "up" else distance
                found.append((data, offset, False, part, column))
                found.append((beside, offset, True, part, column))
            batches.append(found)
        batches[-1:] = [batches[-1][::2], batches[-1][1::2]]
        order = [entry[1:] for found in batches for entry in found]
        table = np.zeros((axis_size, len(order)), np.int32)
        for p, members in enumerate(ring):
            for c, at in enumerate(members):
                for k, (offset, beside, part, column) in enumerate(order):
                    source = ring[(p + offset) % chips][1 - c if beside else c]
                    table[at, k] = (source * device_units + part * half + column) // LANES
        starts = jnp.asarray(table)[me]
        acc = None
        done = 0
        for k, found in enumerate(batches):
            last = k == len(batches) - 1
            acc = chunk_matmul(
                [entry[0] for entry in found],
                starts,
                done,
                weight,
                acc,
                extra if k == len(batches) - 4 else None,
                jnp.bfloat16 if last else jnp.float32,
            )
            done += len(found)
        return acc

    def local(
        gated_hidden_rows,
        down_base_weight,
        adapter_input_factor,
        adapter_output_weight,
        request_adapter_index,
    ):
        steps, requests, device_units = gated_hidden_rows.shape
        total = steps * requests
        fits = device_units % (2 * LANES) == 0 and total % (32 * max(long, 1)) == 0
        run = ringed if snake and cores == 2 and long > 1 and fits else plain
        out = run(
            gated_hidden_rows.reshape(total, device_units),
            down_base_weight,
            adapter_input_factor,
            adapter_output_weight,
            request_adapter_index.reshape(total),
        )
        return out.reshape(steps, requests, out.shape[1])

    placed = (
        P(None, "groups", "row"),
        P("row", None),
        P(None, None, "row"),
        P(None, None, "row"),
        P(None, "groups"),
    )

    return jax.shard_map(
        local, mesh=mesh, in_specs=placed, out_specs=P(None, "groups", "row"), check_vma=False
    )
```

```python
import jax
import jax.numpy as jnp
import numpy as np
from jax import lax
from jax.experimental import pallas as pl
from jax.experimental.pallas import tpu as pltpu
from jax.sharding import PartitionSpec as P


LANES = 128


def chip_ring(mesh):
    line = mesh.devices.reshape(mesh.devices.shape[0], -1)[0]
    chips = {}
    for at, device in enumerate(line):
        place = tuple(getattr(device, "coords", (at, 0, 0)))
        chips.setdefault(place, []).append(at)
    places = list(chips)
    if len({len(c) for c in chips.values()}) != 1:
        return [[at] for at in range(len(line))], False
    used = [k for k in range(len(places[0])) if len({p[k] for p in places}) > 1]
    if len(used) == 2:
        sizes = [len({p[k] for p in places}) for k in used]
        if 2 in sizes and sizes[0] * sizes[1] == len(places):
            short = used[sizes.index(2)]
            long = used[0] if short == used[1] else used[1]
            low = min(p[short] for p in places)
            up = sorted((p for p in places if p[short] == low), key=lambda p: p[long])
            down = sorted((p for p in places if p[short] != low), key=lambda p: -p[long])
            places = up + down
            return [chips[p] for p in places], True
    return [chips[p] for p in places], False


def in_hbm(array):
    return pltpu.with_memory_space_constraint(array, pltpu.HBM)


def project_selected(rows, labels, factors, first):
    count, rank, units = factors.shape
    total = rows.shape[0]
    wide = count * rank
    part = total // 2

    def body(f_ref, x_ref, l_ref, a_any, mine_ref, other_ref, s_ref, a_ref, sem):
        copy = pltpu.make_async_copy(a_any, a_ref, sem)
        copy.start()
        copy.wait()
        full = lax.dot_general(
            x_ref[...], a_ref[...], (((1,), (1,)), ((), ())), preferred_element_type=jnp.float32
        )
        own = jnp.zeros((total, rank), jnp.float32)
        for k in range(count):
            own = own + jnp.where(l_ref[...] == k, full[:, k * rank : (k + 1) * rank], 0.0)
        s_ref[...] = jnp.concatenate([own, full[:, :rank]], axis=1)
        at = f_ref[0]
        mine_ref[...] = s_ref[pl.ds(pl.multiple_of(at * part, 8), part), :]
        other_ref[...] = s_ref[pl.ds(pl.multiple_of((1 - at) * part, 8), part), :]

    vmem = pl.BlockSpec(memory_space=pltpu.VMEM)
    anywhere = pl.BlockSpec(memory_space=pltpu.HBM)
    shape = jax.ShapeDtypeStruct((part, 2 * rank), jnp.float32)
    return pl.pallas_call(
        body,
        out_shape=(shape, shape),
        in_specs=[pl.BlockSpec(memory_space=pltpu.SMEM), vmem, vmem, anywhere],
        out_specs=(vmem, vmem),
        scratch_shapes=[
            pltpu.VMEM((total, 2 * rank), jnp.float32),
            pltpu.VMEM((wide, units), jnp.bfloat16),
            pltpu.SemaphoreType.DMA,
        ],
        cost_estimate=pl.CostEstimate(
            flops=2 * total * wide * units,
            transcendentals=0,
            bytes_accessed=2 * units * (total + wide) + 8 * total * rank,
        ),
        compiler_params=pltpu.CompilerParams(vmem_limit_bytes=12 << 20),
    )(first.reshape(1), rows, labels[:, None], in_hbm(factors.reshape(wide, units)))


def labels_onehot(adapter_labels, count):
    return adapter_labels[:, None] == jnp.arange(count, dtype=jnp.int32)[None, :]


def select_both(project_rows, adapter_labels, count, rank):
    choose = labels_onehot(adapter_labels, count).astype(jnp.float32)
    total = project_rows.shape[0]
    own = jnp.sum(project_rows.reshape(total, count, rank) * choose[:, :, None], axis=1)
    return jnp.concatenate([own, project_rows[:, :rank]], axis=1)


def expand_factor(shrunk_rows, adapter_labels, adapter_output_weight):
    count, rank, width = adapter_output_weight.shape
    total = shrunk_rows.shape[0]
    choose = labels_onehot(adapter_labels, count).astype(jnp.float32)
    spread = (choose[:, :, None] * shrunk_rows[:, None, :rank].astype(jnp.float32)).reshape(
        total, count * rank
    )
    operand = jnp.concatenate([spread.astype(jnp.bfloat16), shrunk_rows[:, rank:]], axis=1)
    stacked = jnp.concatenate(
        [adapter_output_weight.reshape(count * rank, width), -adapter_output_weight[0]], axis=0
    )
    return jnp.dot(operand, stacked, preferred_element_type=jnp.float32)


def adapter_terms(summed, labels, outputs):
    rank = outputs.shape[1]
    keep = (labels != 0).astype(jnp.float32)[:, None]
    shrunk_rows = (summed * keep).astype(jnp.bfloat16)
    resident = jnp.dot(
        summed[:, rank:], outputs[0].astype(jnp.float32), precision=lax.Precision.HIGHEST
    )
    return resident + expand_factor(shrunk_rows, labels, outputs)


def sum_over_row(summand, axis_size):
    rows, cols = summand.shape
    if rows % axis_size:
        return lax.psum(summand, "row")
    parts = lax.all_to_all(summand, "row", 0, 0, tiled=True)
    mine = jnp.sum(parts.reshape(axis_size, rows // axis_size, cols), axis=0)
    spread = jnp.broadcast_to(mine[None], (axis_size,) + mine.shape).reshape(rows, cols)
    return lax.all_to_all(spread, "row", 0, 0, tiled=True)


def swap(rows, at, pairs):
    part = rows.shape[0] // 2
    low, high = rows[:part], rows[part:]
    got = lax.ppermute(jnp.where(at == 0, high, low), "row", pairs)
    return jnp.where(at == 0, low, high) + got


def join(part, at, pairs):
    got = lax.ppermute(part, "row", pairs)
    return jnp.concatenate([jnp.where(at == 0, part, got), jnp.where(at == 0, got, part)], axis=0)


def sum_by_stages(mine, other, side, partner, across, lines):
    got = lax.ppermute(other, "row", partner)
    rows = swap(mine + got, side, across)
    size = len(lines[0])
    piece = rows.shape[0] // size
    parts = lax.all_to_all(rows, "row", 0, 0, axis_index_groups=lines, tiled=True)
    total = jnp.sum(parts.reshape(size, piece, rows.shape[1]), axis=0)
    spread = jnp.broadcast_to(total[None], (size,) + total.shape).reshape(rows.shape)
    whole = lax.all_to_all(spread, "row", 0, 0, axis_index_groups=lines, tiled=True)
    half = join(whole, side, across)
    return half, lax.ppermute(half, "row", partner)


def chunk_matmul(chunks, starts, first, weight, added, out_dtype, ready=None, ahead=()):
    count = len(chunks)
    rows = chunks[0].shape[0]
    widths = [c.shape[1] for c in chunks]
    features = weight.shape[0]
    later = len(ahead)

    def body(starts_ref, *refs):
        x_refs, refs = refs[:count], refs[count:]
        w_refs, refs = refs[: len(blocks)], refs[len(blocks) :]
        add_refs, refs = refs[: len(added)], refs[len(added) :]
        out_ref, ahead_refs, refs = refs[0], refs[1 : 1 + later], refs[1 + later :]

        def block(at, units):
            start = pl.multiple_of(starts_ref[at] * LANES, LANES)
            return w_refs[0].at[:, pl.ds(start, units)]

        copies = []
        w_bufs = w_refs
        if ready is None:
            w_bufs, w_sem = refs[:count], refs[count]
            for k in range(count):
                copy = pltpu.make_async_copy(block(first + k, widths[k]), w_bufs[k], w_sem.at[k])
                copy.start()
                copies.append(copy)
        fetches = [
            pltpu.make_async_copy(block(at, units), ahead_refs[k], refs[-1].at[k])
            for k, (at, units) in enumerate(ahead)
        ]
        for fetch in fetches:
            fetch.start()
        total = None
        for k in range(count):
            if copies:
                copies[k].wait()
            part = lax.dot_general(
                x_refs[k][...],
                w_bufs[k][...],
                (((1,), (1,)), ((), ())),
                preferred_element_type=jnp.float32,
            )
            total = part if total is None else total + part
        for ref in add_refs:
            total = total + ref[...]
        out_ref[...] = total.astype(out_dtype)
        for fetch in fetches:
            fetch.wait()

    anywhere = pl.BlockSpec(memory_space=pltpu.HBM)
    vmem = pl.BlockSpec(memory_space=pltpu.VMEM)
    blocks = [in_hbm(weight)] if ready is None else list(ready)
    held = anywhere if ready is None else vmem
    scratch = []
    if ready is None:
        scratch += [pltpu.VMEM((features, w), jnp.bfloat16) for w in widths]
        scratch += [pltpu.SemaphoreType.DMA((count,))]
    if later:
        scratch += [pltpu.SemaphoreType.DMA((later,))]
    room = 2 * sum(widths) * (rows + features) + 2 * features * sum(u for _, u in ahead)
    room += 4 * rows * features * (1 + len(added))
    moved = sum(widths) * (rows + features) + features * sum(units for _, units in ahead)
    out = pl.pallas_call(
        body,
        out_shape=[jax.ShapeDtypeStruct((rows, features), out_dtype)]
        + [jax.ShapeDtypeStruct((features, units), jnp.bfloat16) for _, units in ahead],
        in_specs=[pl.BlockSpec(memory_space=pltpu.SMEM)]
        + [vmem] * count
        + [held] * len(blocks)
        + [vmem] * len(added),
        out_specs=[vmem] * (1 + later),
        scratch_shapes=scratch,
        cost_estimate=pl.CostEstimate(
            flops=2 * rows * sum(widths) * features,
            transcendentals=0,
            bytes_accessed=2 * moved + 8 * rows * features,
        ),
        compiler_params=pltpu.CompilerParams(vmem_limit_bytes=room + (5 << 20)),
    )(starts, *chunks, *blocks, *added)
    return out[0], out[1:]


def adapter_kernel(mine, other, core, labels, outputs):
    count, rank, width = outputs.shape
    part, cols = mine.shape
    total = 2 * part

    def body(core_ref, mine_ref, other_ref, l_ref, w_ref, o_ref, s_ref):
        at = core_ref[0]
        s_ref[pl.ds(pl.multiple_of(at * part, 8), part), :] = mine_ref[...]
        s_ref[pl.ds(pl.multiple_of((1 - at) * part, 8), part), :] = other_ref[...]
        summed = s_ref[...]
        label = l_ref[...]
        shrunk = jnp.where(label != 0, summed, 0.0).astype(jnp.bfloat16).astype(jnp.float32)
        own = shrunk[:, :rank]
        spread = jnp.concatenate([jnp.where(label == k, own, 0.0) for k in range(count)], axis=1)
        update = jnp.dot(
            spread.astype(jnp.bfloat16), w_ref[...], preferred_element_type=jnp.float32
        )
        resident = summed[:, rank:]
        high = resident.astype(jnp.bfloat16)
        left = resident - high.astype(jnp.float32)
        middle = left.astype(jnp.bfloat16)
        low = (left - middle.astype(jnp.float32)).astype(jnp.bfloat16)
        first = w_ref[:rank, :]
        taken = shrunk[:, rank:].astype(jnp.bfloat16)
        base = jnp.dot(low, first, preferred_element_type=jnp.float32)
        base = base + jnp.dot(middle, first, preferred_element_type=jnp.float32)
        base = base + jnp.dot(high, first, preferred_element_type=jnp.float32)
        o_ref[...] = base + (update - jnp.dot(taken, first, preferred_element_type=jnp.float32))

    vmem = pl.BlockSpec(memory_space=pltpu.VMEM)
    return pl.pallas_call(
        body,
        out_shape=jax.ShapeDtypeStruct((total, width), jnp.float32),
        in_specs=[pl.BlockSpec(memory_space=pltpu.SMEM)] + [vmem] * 4,
        out_specs=vmem,
        scratch_shapes=[pltpu.VMEM((total, cols), jnp.float32)],
        cost_estimate=pl.CostEstimate(
            flops=2 * total * (count + 4) * rank * width,
            transcendentals=0,
            bytes_accessed=2 * count * rank * width + 4 * total * (cols + width),
        ),
        compiler_params=pltpu.CompilerParams(vmem_limit_bytes=12 << 20),
    )(core.reshape(1), mine, other, labels[:, None], outputs.reshape(count * rank, width))


def solution(mesh):
    axis_size = mesh.shape["row"]
    ring, snake = chip_ring(mesh)
    chips, cores = len(ring), len(ring[0])
    forward = [(ring[p][c], ring[(p + 1) % chips][c]) for p in range(chips) for c in range(cores)]
    backward = [(b, a) for a, b in forward]
    partner = [(members[c], members[1 - c]) for members in ring for c in range(cores)] if cores == 2 else []

    long = chips // 2
    across = [(ring[p][c], ring[chips - 1 - p][c]) for p in range(chips) for c in range(cores)]
    lines = [
        [ring[p][c] for p in range(lo, lo + long)] for lo in (0, long) for c in range(cores)
    ]
    place = np.zeros((axis_size, 2), np.int32)
    for p, members in enumerate(ring):
        for c, at in enumerate(members):
            place[at] = c, int(p >= long)

    def plain(flat, weight, factors, outputs, labels):
        count, rank, units = factors.shape
        project_rows = jnp.dot(
            flat, factors.reshape(count * rank, units).T, preferred_element_type=jnp.float32
        )
        summed = sum_over_row(select_both(project_rows, labels, count, rank), axis_size)
        base = lax.dot_general(
            lax.all_gather(flat, "row", axis=1, tiled=True),
            weight,
            (((1,), (1,)), ((), ())),
            preferred_element_type=jnp.float32,
        )
        return (base + adapter_terms(summed, labels, outputs)).astype(jnp.bfloat16)

    def ringed(flat, weight, factors, outputs, labels):
        device_units = flat.shape[1]
        half = device_units // 2
        tiles = half // LANES
        cut = (tiles - tiles * 3 // 7) * LANES
        me = lax.axis_index("row")
        core, side = [jnp.asarray(place)[me][k] for k in range(2)]
        mine, other = project_selected(flat, labels, factors, core)
        halves = sum_by_stages(mine, other, side, partner, across, lines)
        extra = adapter_kernel(*halves, core, labels, outputs)

        plan = [(s // 2 + 1, s % 2, 0, half) for s in range(2 * long - 2)]
        plan += [(long, 0, 0, cut), (long, 0, cut, half - cut)]
        own = [flat[:, :half], flat[:, half:]]
        beside = lax.ppermute(flat, "row", partner)
        batches = [[(flat, 0, False, 0, 0), (beside, 0, True, 0, 0)]]
        held = {"up": list(own), "down": list(own)}
        for distance, turn, column, width in plan:
            found = []
            for way, pairs, part in (("up", forward, turn), ("down", backward, 1 - turn)):
                send = held[way][part]
                if width < half:
                    send = send[:, column : column + width]
                data = lax.ppermute(send, "row", pairs)
                if width == half:
                    held[way][part] = data
                beside = lax.ppermute(data, "row", partner)
                offset = -distance if way == "up" else distance
                found.append((data, offset, False, part, column))
                found.append((beside, offset, True, part, column))
            batches.append(found)
        batches[-1:] = [batches[-1][::2], batches[-1][1::2]]
        order = [entry[1:] for found in batches for entry in found]
        table = np.zeros((axis_size, len(order)), np.int32)
        for p, members in enumerate(ring):
            for c, at in enumerate(members):
                for k, (offset, beside, part, column) in enumerate(order):
                    source = ring[(p + offset) % chips][1 - c if beside else c]
                    table[at, k] = (source * device_units + part * half + column) // LANES
        starts = jnp.asarray(table)[me]
        acc = []
        done = 0
        ends = len(batches) - 2
        tail = len(order) - sum(len(found) for found in batches[ends:])
        ahead = [(tail + k, found[0].shape[1]) for k, found in enumerate(batches[ends] + batches[-1])]
        ready = None
        for k, found in enumerate(batches):
            last = k == len(batches) - 1
            held = None
            if k >= ends:
                held, ready = ready[: len(found)], ready[len(found) :]
            out, fetched = chunk_matmul(
                [entry[0] for entry in found],
                starts,
                done,
                weight,
                acc + ([extra] if k == ends - 2 else []),
                jnp.bfloat16 if last else jnp.float32,
                held,
                ahead if k == ends - 1 else (),
            )
            if k == ends - 1:
                ready = fetched
            acc = [out]
            done += len(found)
        return acc[0]

    def local(
        gated_hidden_rows,
        down_base_weight,
        adapter_input_factor,
        adapter_output_weight,
        request_adapter_index,
    ):
        steps, requests, device_units = gated_hidden_rows.shape
        total = steps * requests
        fits = device_units % (2 * LANES) == 0 and total % (32 * max(long, 1)) == 0
        run = ringed if snake and cores == 2 and long > 1 and fits else plain
        out = run(
            gated_hidden_rows.reshape(total, device_units),
            down_base_weight,
            adapter_input_factor,
            adapter_output_weight,
            request_adapter_index.reshape(total),
        )
        return out.reshape(steps, requests, out.shape[1])

    placed = (
        P(None, "groups", "row"),
        P("row", None),
        P(None, None, "row"),
        P(None, None, "row"),
        P(None, "groups"),
    )

    return jax.shard_map(
        local, mesh=mesh, in_specs=placed, out_specs=P(None, "groups", "row"), check_vma=False
    )
```

```python
import jax
import jax.numpy as jnp
import numpy as np
from jax import lax
from jax.experimental import pallas as pl
from jax.experimental.pallas import tpu as pltpu
from jax.sharding import PartitionSpec as P


LANES = 128


def chip_ring(mesh):
    line = mesh.devices.reshape(mesh.devices.shape[0], -1)[0]
    chips = {}
    for at, device in enumerate(line):
        place = tuple(getattr(device, "coords", (at, 0, 0)))
        chips.setdefault(place, []).append(at)
    places = list(chips)
    if len({len(c) for c in chips.values()}) != 1:
        return [[at] for at in range(len(line))], False
    used = [k for k in range(len(places[0])) if len({p[k] for p in places}) > 1]
    if len(used) == 2:
        sizes = [len({p[k] for p in places}) for k in used]
        if 2 in sizes and sizes[0] * sizes[1] == len(places):
            short = used[sizes.index(2)]
            long = used[0] if short == used[1] else used[1]
            low = min(p[short] for p in places)
            up = sorted((p for p in places if p[short] == low), key=lambda p: p[long])
            down = sorted((p for p in places if p[short] != low), key=lambda p: -p[long])
            places = up + down
            return [chips[p] for p in places], True
    return [chips[p] for p in places], False


def in_hbm(array):
    return pltpu.with_memory_space_constraint(array, pltpu.HBM)


def cut_block(block, half):
    def body(x_ref, a_ref, b_ref, sem):
        copies = [
            pltpu.make_async_copy(x_ref.at[:, pl.ds(k * half, half)], out, sem.at[k])
            for k, out in enumerate((a_ref, b_ref))
        ]
        for copy in copies:
            copy.start()
        for copy in copies:
            copy.wait()

    vmem = pl.BlockSpec(memory_space=pltpu.VMEM)
    shape = jax.ShapeDtypeStruct((block.shape[0], half), block.dtype)
    return pl.pallas_call(
        body,
        out_shape=(shape, shape),
        in_specs=[pl.BlockSpec(memory_space=pltpu.HBM)],
        out_specs=(vmem, vmem),
        scratch_shapes=[pltpu.SemaphoreType.DMA((2,))],
        compiler_params=pltpu.CompilerParams(vmem_limit_bytes=4 << 20),
    )(in_hbm(block))


def project_selected(rows, labels, factors, first):
    count, rank, units = factors.shape
    total = rows[0].shape[0]
    half = units // 2
    wide = count * rank
    part = total // 2

    def body(f_ref, low_ref, high_ref, l_ref, a_any, mine_ref, other_ref, s_ref, a_ref, sem):
        copy = pltpu.make_async_copy(a_any, a_ref, sem)
        copy.start()
        copy.wait()
        full = sum(
            lax.dot_general(
                x_ref[...],
                a_ref[:, k * half : (k + 1) * half],
                (((1,), (1,)), ((), ())),
                preferred_element_type=jnp.float32,
            )
            for k, x_ref in enumerate((low_ref, high_ref))
        )
        own = jnp.zeros((total, rank), jnp.float32)
        for k in range(count):
            own = own + jnp.where(l_ref[...] == k, full[:, k * rank : (k + 1) * rank], 0.0)
        s_ref[...] = jnp.concatenate([own, full[:, :rank]], axis=1)
        at = f_ref[0]
        mine_ref[...] = s_ref[pl.ds(pl.multiple_of(at * part, 8), part), :]
        other_ref[...] = s_ref[pl.ds(pl.multiple_of((1 - at) * part, 8), part), :]

    vmem = pl.BlockSpec(memory_space=pltpu.VMEM)
    anywhere = pl.BlockSpec(memory_space=pltpu.HBM)
    shape = jax.ShapeDtypeStruct((part, 2 * rank), jnp.float32)
    return pl.pallas_call(
        body,
        out_shape=(shape, shape),
        in_specs=[pl.BlockSpec(memory_space=pltpu.SMEM), vmem, vmem, vmem, anywhere],
        out_specs=(vmem, vmem),
        scratch_shapes=[
            pltpu.VMEM((total, 2 * rank), jnp.float32),
            pltpu.VMEM((wide, units), jnp.bfloat16),
            pltpu.SemaphoreType.DMA,
        ],
        cost_estimate=pl.CostEstimate(
            flops=2 * total * wide * units,
            transcendentals=0,
            bytes_accessed=2 * units * (total + wide) + 8 * total * rank,
        ),
        compiler_params=pltpu.CompilerParams(vmem_limit_bytes=12 << 20),
    )(first.reshape(1), *rows, labels[:, None], in_hbm(factors.reshape(wide, units)))


def labels_onehot(adapter_labels, count):
    return adapter_labels[:, None] == jnp.arange(count, dtype=jnp.int32)[None, :]


def select_both(project_rows, adapter_labels, count, rank):
    choose = labels_onehot(adapter_labels, count).astype(jnp.float32)
    total = project_rows.shape[0]
    own = jnp.sum(project_rows.reshape(total, count, rank) * choose[:, :, None], axis=1)
    return jnp.concatenate([own, project_rows[:, :rank]], axis=1)


def expand_factor(shrunk_rows, adapter_labels, adapter_output_weight):
    count, rank, width = adapter_output_weight.shape
    total = shrunk_rows.shape[0]
    choose = labels_onehot(adapter_labels, count).astype(jnp.float32)
    spread = (choose[:, :, None] * shrunk_rows[:, None, :rank].astype(jnp.float32)).reshape(
        total, count * rank
    )
    operand = jnp.concatenate([spread.astype(jnp.bfloat16), shrunk_rows[:, rank:]], axis=1)
    stacked = jnp.concatenate(
        [adapter_output_weight.reshape(count * rank, width), -adapter_output_weight[0]], axis=0
    )
    return jnp.dot(operand, stacked, preferred_element_type=jnp.float32)


def adapter_terms(summed, labels, outputs):
    rank = outputs.shape[1]
    keep = (labels != 0).astype(jnp.float32)[:, None]
    shrunk_rows = (summed * keep).astype(jnp.bfloat16)
    resident = jnp.dot(
        summed[:, rank:], outputs[0].astype(jnp.float32), precision=lax.Precision.HIGHEST
    )
    return resident + expand_factor(shrunk_rows, labels, outputs)


def sum_over_row(summand, axis_size):
    rows, cols = summand.shape
    if rows % axis_size:
        return lax.psum(summand, "row")
    parts = lax.all_to_all(summand, "row", 0, 0, tiled=True)
    mine = jnp.sum(parts.reshape(axis_size, rows // axis_size, cols), axis=0)
    spread = jnp.broadcast_to(mine[None], (axis_size,) + mine.shape).reshape(rows, cols)
    return lax.all_to_all(spread, "row", 0, 0, tiled=True)


def swap(rows, at, pairs):
    part = rows.shape[0] // 2
    low, high = rows[:part], rows[part:]
    got = lax.ppermute(jnp.where(at == 0, high, low), "row", pairs)
    return jnp.where(at == 0, low, high) + got


def join(part, at, pairs):
    got = lax.ppermute(part, "row", pairs)
    return jnp.concatenate([jnp.where(at == 0, part, got), jnp.where(at == 0, got, part)], axis=0)


def sum_by_stages(mine, other, side, partner, across, lines):
    got = lax.ppermute(other, "row", partner)
    rows = swap(mine + got, side, across)
    size = len(lines[0])
    piece = rows.shape[0] // size
    parts = lax.all_to_all(rows, "row", 0, 0, axis_index_groups=lines, tiled=True)
    total = jnp.sum(parts.reshape(size, piece, rows.shape[1]), axis=0)
    spread = jnp.broadcast_to(total[None], (size,) + total.shape).reshape(rows.shape)
    whole = lax.all_to_all(spread, "row", 0, 0, axis_index_groups=lines, tiled=True)
    half = join(whole, side, across)
    return half, lax.ppermute(half, "row", partner)


def chunk_matmul(chunks, starts, first, weight, added, out_dtype, ready, ahead):
    count = len(chunks)
    rows = chunks[0].shape[0]
    widths = [c.shape[1] for c in chunks]
    features = weight.shape[0]
    later = len(ahead)

    def body(starts_ref, *refs):
        x_refs, refs = refs[:count], refs[count:]
        w_any, refs = refs[0], refs[1:]
        w_refs, refs = refs[: len(ready)], refs[len(ready) :]
        add_refs, refs = refs[: len(added)], refs[len(added) :]
        out_ref, ahead_refs, refs = refs[0], refs[1 : 1 + later], refs[1 + later :]

        def block(at, units):
            start = pl.multiple_of(starts_ref[at] * LANES, LANES)
            return w_any.at[:, pl.ds(start, units)]

        copies = []
        if not ready:
            w_refs, w_sem = refs[:count], refs[count]
            for k in range(count):
                copy = pltpu.make_async_copy(block(first + k, widths[k]), w_refs[k], w_sem.at[k])
                copy.start()
                copies.append(copy)
        fetches = [
            pltpu.make_async_copy(block(at, units), ahead_refs[k], refs[-1].at[k])
            for k, (at, units) in enumerate(ahead)
        ]
        for fetch in fetches:
            fetch.start()
        total = None
        for k in range(count):
            if copies:
                copies[k].wait()
            part = lax.dot_general(
                x_refs[k][...],
                w_refs[k][...],
                (((1,), (1,)), ((), ())),
                preferred_element_type=jnp.float32,
            )
            total = part if total is None else total + part
        for ref in add_refs:
            total = total + ref[...]
        out_ref[...] = total.astype(out_dtype)
        for fetch in fetches:
            fetch.wait()

    anywhere = pl.BlockSpec(memory_space=pltpu.HBM)
    vmem = pl.BlockSpec(memory_space=pltpu.VMEM)
    scratch = []
    if not ready:
        scratch += [pltpu.VMEM((features, w), jnp.bfloat16) for w in widths]
        scratch += [pltpu.SemaphoreType.DMA((count,))]
    if later:
        scratch += [pltpu.SemaphoreType.DMA((later,))]
    room = 2 * sum(widths) * (rows + features) + 2 * features * sum(u for _, u in ahead)
    room += 4 * rows * features * (1 + len(added))
    moved = sum(widths) * (rows + features) + features * sum(units for _, units in ahead)
    out = pl.pallas_call(
        body,
        out_shape=[jax.ShapeDtypeStruct((rows, features), out_dtype)]
        + [jax.ShapeDtypeStruct((features, units), jnp.bfloat16) for _, units in ahead],
        in_specs=[pl.BlockSpec(memory_space=pltpu.SMEM)]
        + [vmem] * count
        + [anywhere]
        + [vmem] * (len(ready) + len(added)),
        out_specs=[vmem] * (1 + later),
        scratch_shapes=scratch,
        cost_estimate=pl.CostEstimate(
            flops=2 * rows * sum(widths) * features,
            transcendentals=0,
            bytes_accessed=2 * moved + 8 * rows * features,
        ),
        compiler_params=pltpu.CompilerParams(vmem_limit_bytes=room + (5 << 20)),
    )(starts, *chunks, in_hbm(weight), *ready, *added)
    return out[0], out[1:]


def adapter_kernel(mine, other, core, labels, outputs):
    count, rank, width = outputs.shape
    part, cols = mine.shape
    total = 2 * part

    def body(core_ref, mine_ref, other_ref, l_ref, w_ref, o_ref, s_ref):
        at = core_ref[0]
        s_ref[pl.ds(pl.multiple_of(at * part, 8), part), :] = mine_ref[...]
        s_ref[pl.ds(pl.multiple_of((1 - at) * part, 8), part), :] = other_ref[...]
        summed = s_ref[...]
        label = l_ref[...]
        shrunk = jnp.where(label != 0, summed, 0.0).astype(jnp.bfloat16).astype(jnp.float32)
        own = shrunk[:, :rank]
        spread = jnp.concatenate([jnp.where(label == k, own, 0.0) for k in range(count)], axis=1)
        update = jnp.dot(
            spread.astype(jnp.bfloat16), w_ref[...], preferred_element_type=jnp.float32
        )
        resident = summed[:, rank:]
        high = resident.astype(jnp.bfloat16)
        left = resident - high.astype(jnp.float32)
        middle = left.astype(jnp.bfloat16)
        low = (left - middle.astype(jnp.float32)).astype(jnp.bfloat16)
        first = w_ref[:rank, :]
        taken = shrunk[:, rank:].astype(jnp.bfloat16)
        base = jnp.dot(low, first, preferred_element_type=jnp.float32)
        base = base + jnp.dot(middle, first, preferred_element_type=jnp.float32)
        base = base + jnp.dot(high, first, preferred_element_type=jnp.float32)
        o_ref[...] = base + (update - jnp.dot(taken, first, preferred_element_type=jnp.float32))

    vmem = pl.BlockSpec(memory_space=pltpu.VMEM)
    return pl.pallas_call(
        body,
        out_shape=jax.ShapeDtypeStruct((total, width), jnp.float32),
        in_specs=[pl.BlockSpec(memory_space=pltpu.SMEM)] + [vmem] * 4,
        out_specs=vmem,
        scratch_shapes=[pltpu.VMEM((total, cols), jnp.float32)],
        cost_estimate=pl.CostEstimate(
            flops=2 * total * (count + 4) * rank * width,
            transcendentals=0,
            bytes_accessed=2 * count * rank * width + 4 * total * (cols + width),
        ),
        compiler_params=pltpu.CompilerParams(vmem_limit_bytes=12 << 20),
    )(core.reshape(1), mine, other, labels[:, None], outputs.reshape(count * rank, width))


def solution(mesh):
    axis_size = mesh.shape["row"]
    ring, snake = chip_ring(mesh)
    chips, cores = len(ring), len(ring[0])
    forward = [(ring[p][c], ring[(p + 1) % chips][c]) for p in range(chips) for c in range(cores)]
    backward = [(b, a) for a, b in forward]
    partner = [(members[c], members[1 - c]) for members in ring for c in range(cores)] if cores == 2 else []

    long = chips // 2
    across = [(ring[p][c], ring[chips - 1 - p][c]) for p in range(chips) for c in range(cores)]
    lines = [
        [ring[p][c] for p in range(lo, lo + long)] for lo in (0, long) for c in range(cores)
    ]
    place = np.zeros((axis_size, 2), np.int32)
    for p, members in enumerate(ring):
        for c, at in enumerate(members):
            place[at] = c, int(p >= long)

    def plain(flat, weight, factors, outputs, labels):
        count, rank, units = factors.shape
        project_rows = jnp.dot(
            flat, factors.reshape(count * rank, units).T, preferred_element_type=jnp.float32
        )
        summed = sum_over_row(select_both(project_rows, labels, count, rank), axis_size)
        base = lax.dot_general(
            lax.all_gather(flat, "row", axis=1, tiled=True),
            weight,
            (((1,), (1,)), ((), ())),
            preferred_element_type=jnp.float32,
        )
        return (base + adapter_terms(summed, labels, outputs)).astype(jnp.bfloat16)

    def ringed(flat, weight, factors, outputs, labels):
        device_units = flat.shape[1]
        half = device_units // 2
        tiles = half // LANES
        cut = (tiles - tiles * 2 // 7) * LANES
        me = lax.axis_index("row")
        core, side = [jnp.asarray(place)[me][k] for k in range(2)]
        own = cut_block(flat, half)
        mine, other = project_selected(own, labels, factors, core)
        halves = sum_by_stages(mine, other, side, partner, across, lines)
        extra = adapter_kernel(*halves, core, labels, outputs)

        plan = [(s // 2 + 1, s % 2, 0, half) for s in range(2 * long - 2)]
        plan += [(long, 0, 0, cut), (long, 0, cut, half - cut)]
        beside = lax.ppermute(flat, "row", partner)
        batches = [[(own[part], 0, False, part, 0) for part in range(2)] + [(beside, 0, True, 0, 0)]]
        held = {"up": list(own), "down": list(own)}
        for distance, turn, column, width in plan:
            found = []
            for way, pairs, part in (("up", forward, turn), ("down", backward, 1 - turn)):
                send = held[way][part]
                if width < half:
                    send = send[:, column : column + width]
                data = lax.ppermute(send, "row", pairs)
                if width == half:
                    held[way][part] = data
                beside = lax.ppermute(data, "row", partner)
                offset = -distance if way == "up" else distance
                found.append((data, offset, False, part, column))
                found.append((beside, offset, True, part, column))
            batches.append(found)
        batches[-1:] = [batches[-1][::2], batches[-1][1::2]]
        order = [entry[1:] for found in batches for entry in found]
        table = np.zeros((axis_size, len(order)), np.int32)
        for p, members in enumerate(ring):
            for c, at in enumerate(members):
                for k, (offset, beside, part, column) in enumerate(order):
                    source = ring[(p + offset) % chips][1 - c if beside else c]
                    table[at, k] = (source * device_units + part * half + column) // LANES
        starts = jnp.asarray(table)[me]
        acc, ready, done = [], [], 0
        ends = len(batches) - 2
        settled = min(3, ends - 2)
        for k, found in enumerate(batches):
            last = k == len(batches) - 1
            coming = []
            if settled <= k <= ends - 2:
                coming = batches[k + 1] if k < ends - 2 else sum(batches[k + 1 :], [])
            at = done + len(found)
            ahead = [(at + j, entry[0].shape[1]) for j, entry in enumerate(coming)]
            out, fetched = chunk_matmul(
                [entry[0] for entry in found],
                starts,
                done,
                weight,
                acc + ([extra] if k == ends - 2 else []),
                jnp.bfloat16 if last else jnp.float32,
                ready[: len(found)],
                ahead,
            )
            ready = ready[len(found) :] + list(fetched)
            acc = [out]
            done += len(found)
        return acc[0]

    def local(
        gated_hidden_rows,
        down_base_weight,
        adapter_input_factor,
        adapter_output_weight,
        request_adapter_index,
    ):
        steps, requests, device_units = gated_hidden_rows.shape
        total = steps * requests
        fits = device_units % (2 * LANES) == 0 and total % (32 * max(long, 1)) == 0
        run = ringed if snake and cores == 2 and long > 1 and fits else plain
        out = run(
            gated_hidden_rows.reshape(total, device_units),
            down_base_weight,
            adapter_input_factor,
            adapter_output_weight,
            request_adapter_index.reshape(total),
        )
        return out.reshape(steps, requests, out.shape[1])

    placed = (
        P(None, "groups", "row"),
        P("row", None),
        P(None, None, "row"),
        P(None, None, "row"),
        P(None, "groups"),
    )

    return jax.shard_map(
        local, mesh=mesh, in_specs=placed, out_specs=P(None, "groups", "row"), check_vma=False
    )
```

```python
import jax
import jax.numpy as jnp
import numpy as np
from jax import lax
from jax.experimental import pallas as pl
from jax.experimental.pallas import tpu as pltpu
from jax.sharding import PartitionSpec as P


LANES = 128


def chip_ring(mesh):
    line = mesh.devices.reshape(mesh.devices.shape[0], -1)[0]
    chips = {}
    for at, device in enumerate(line):
        place = tuple(getattr(device, "coords", (at, 0, 0)))
        chips.setdefault(place, []).append(at)
    places = list(chips)
    if len({len(c) for c in chips.values()}) != 1:
        return [[at] for at in range(len(line))], False
    used = [k for k in range(len(places[0])) if len({p[k] for p in places}) > 1]
    if len(used) == 2:
        sizes = [len({p[k] for p in places}) for k in used]
        if 2 in sizes and sizes[0] * sizes[1] == len(places):
            short = used[sizes.index(2)]
            long = used[0] if short == used[1] else used[1]
            low = min(p[short] for p in places)
            up = sorted((p for p in places if p[short] == low), key=lambda p: p[long])
            down = sorted((p for p in places if p[short] != low), key=lambda p: -p[long])
            places = up + down
            return [chips[p] for p in places], True
    return [chips[p] for p in places], False


def in_hbm(array):
    return pltpu.with_memory_space_constraint(array, pltpu.HBM)


def cut_block(block, half):
    def body(x_ref, a_ref, b_ref, sem):
        copies = [
            pltpu.make_async_copy(x_ref.at[:, pl.ds(k * half, half)], out, sem.at[k])
            for k, out in enumerate((a_ref, b_ref))
        ]
        for copy in copies:
            copy.start()
        for copy in copies:
            copy.wait()

    vmem = pl.BlockSpec(memory_space=pltpu.VMEM)
    shape = jax.ShapeDtypeStruct((block.shape[0], half), block.dtype)
    return pl.pallas_call(
        body,
        out_shape=(shape, shape),
        in_specs=[pl.BlockSpec(memory_space=pltpu.HBM)],
        out_specs=(vmem, vmem),
        scratch_shapes=[pltpu.SemaphoreType.DMA((2,))],
        compiler_params=pltpu.CompilerParams(vmem_limit_bytes=4 << 20),
    )(in_hbm(block))


def project_selected(rows, labels, factors, first):
    count, rank, units = factors.shape
    total = rows[0].shape[0]
    half = units // 2
    wide = count * rank
    part = total // 2

    def body(f_ref, low_ref, high_ref, l_ref, a_any, mine_ref, other_ref, s_ref, a_ref, sem):
        copy = pltpu.make_async_copy(a_any, a_ref, sem)
        copy.start()
        copy.wait()
        full = sum(
            lax.dot_general(
                x_ref[...],
                a_ref[:, k * half : (k + 1) * half],
                (((1,), (1,)), ((), ())),
                preferred_element_type=jnp.float32,
            )
            for k, x_ref in enumerate((low_ref, high_ref))
        )
        own = jnp.zeros((total, rank), jnp.float32)
        for k in range(count):
            own = own + jnp.where(l_ref[...] == k, full[:, k * rank : (k + 1) * rank], 0.0)
        s_ref[...] = jnp.concatenate([own, full[:, :rank]], axis=1)
        at = f_ref[0]
        mine_ref[...] = s_ref[pl.ds(pl.multiple_of(at * part, 8), part), :]
        other_ref[...] = s_ref[pl.ds(pl.multiple_of((1 - at) * part, 8), part), :]

    vmem = pl.BlockSpec(memory_space=pltpu.VMEM)
    anywhere = pl.BlockSpec(memory_space=pltpu.HBM)
    shape = jax.ShapeDtypeStruct((part, 2 * rank), jnp.float32)
    return pl.pallas_call(
        body,
        out_shape=(shape, shape),
        in_specs=[pl.BlockSpec(memory_space=pltpu.SMEM), vmem, vmem, vmem, anywhere],
        out_specs=(vmem, vmem),
        scratch_shapes=[
            pltpu.VMEM((total, 2 * rank), jnp.float32),
            pltpu.VMEM((wide, units), jnp.bfloat16),
            pltpu.SemaphoreType.DMA,
        ],
        cost_estimate=pl.CostEstimate(
            flops=2 * total * wide * units,
            transcendentals=0,
            bytes_accessed=2 * units * (total + wide) + 8 * total * rank,
        ),
        compiler_params=pltpu.CompilerParams(vmem_limit_bytes=12 << 20),
    )(first.reshape(1), *rows, labels[:, None], in_hbm(factors.reshape(wide, units)))


def labels_onehot(adapter_labels, count):
    return adapter_labels[:, None] == jnp.arange(count, dtype=jnp.int32)[None, :]


def select_both(project_rows, adapter_labels, count, rank):
    choose = labels_onehot(adapter_labels, count).astype(jnp.float32)
    total = project_rows.shape[0]
    own = jnp.sum(project_rows.reshape(total, count, rank) * choose[:, :, None], axis=1)
    return jnp.concatenate([own, project_rows[:, :rank]], axis=1)


def expand_factor(shrunk_rows, adapter_labels, adapter_output_weight):
    count, rank, width = adapter_output_weight.shape
    total = shrunk_rows.shape[0]
    choose = labels_onehot(adapter_labels, count).astype(jnp.float32)
    spread = (choose[:, :, None] * shrunk_rows[:, None, :rank].astype(jnp.float32)).reshape(
        total, count * rank
    )
    operand = jnp.concatenate([spread.astype(jnp.bfloat16), shrunk_rows[:, rank:]], axis=1)
    stacked = jnp.concatenate(
        [adapter_output_weight.reshape(count * rank, width), -adapter_output_weight[0]], axis=0
    )
    return jnp.dot(operand, stacked, preferred_element_type=jnp.float32)


def adapter_terms(summed, labels, outputs):
    rank = outputs.shape[1]
    keep = (labels != 0).astype(jnp.float32)[:, None]
    shrunk_rows = (summed * keep).astype(jnp.bfloat16)
    resident = jnp.dot(
        summed[:, rank:], outputs[0].astype(jnp.float32), precision=lax.Precision.HIGHEST
    )
    return resident + expand_factor(shrunk_rows, labels, outputs)


def sum_over_row(summand, axis_size):
    rows, cols = summand.shape
    if rows % axis_size:
        return lax.psum(summand, "row")
    parts = lax.all_to_all(summand, "row", 0, 0, tiled=True)
    mine = jnp.sum(parts.reshape(axis_size, rows // axis_size, cols), axis=0)
    spread = jnp.broadcast_to(mine[None], (axis_size,) + mine.shape).reshape(rows, cols)
    return lax.all_to_all(spread, "row", 0, 0, tiled=True)


def swap(rows, at, pairs):
    part = rows.shape[0] // 2
    low, high = rows[:part], rows[part:]
    got = lax.ppermute(jnp.where(at == 0, high, low), "row", pairs)
    return jnp.where(at == 0, low, high) + got


def join(part, at, pairs):
    got = lax.ppermute(part, "row", pairs)
    return jnp.concatenate([jnp.where(at == 0, part, got), jnp.where(at == 0, got, part)], axis=0)


def sum_by_stages(mine, other, side, partner, across, lines):
    got = lax.ppermute(other, "row", partner)
    rows = swap(mine + got, side, across)
    size = len(lines[0])
    piece = rows.shape[0] // size
    parts = lax.all_to_all(rows, "row", 0, 0, axis_index_groups=lines, tiled=True)
    total = jnp.sum(parts.reshape(size, piece, rows.shape[1]), axis=0)
    spread = jnp.broadcast_to(total[None], (size,) + total.shape).reshape(rows.shape)
    whole = lax.all_to_all(spread, "row", 0, 0, axis_index_groups=lines, tiled=True)
    half = join(whole, side, across)
    return half, lax.ppermute(half, "row", partner)


def chunk_matmul(chunks, starts, first, weight, added, out_dtype, ready, ahead):
    count = len(chunks)
    rows = chunks[0].shape[0]
    widths = [c.shape[1] for c in chunks]
    features = weight.shape[0]
    later = len(ahead)

    def body(starts_ref, *refs):
        x_refs, refs = refs[:count], refs[count:]
        w_any, refs = refs[0], refs[1:]
        w_refs, refs = refs[: len(ready)], refs[len(ready) :]
        add_refs, refs = refs[: len(added)], refs[len(added) :]
        out_ref, ahead_refs, refs = refs[0], refs[1 : 1 + later], refs[1 + later :]

        def block(at, units):
            start = pl.multiple_of(starts_ref[at] * LANES, LANES)
            return w_any.at[:, pl.ds(start, units)]

        copies = []
        if not ready:
            w_refs, w_sem = refs[:count], refs[count]
            for k in range(count):
                copy = pltpu.make_async_copy(block(first + k, widths[k]), w_refs[k], w_sem.at[k])
                copy.start()
                copies.append(copy)
        fetches = [
            pltpu.make_async_copy(block(at, units), ahead_refs[k], refs[-1].at[k])
            for k, (at, units) in enumerate(ahead)
        ]
        for fetch in fetches:
            fetch.start()
        total = None
        for k in range(count):
            if copies:
                copies[k].wait()
            part = lax.dot_general(
                x_refs[k][...],
                w_refs[k][...],
                (((1,), (1,)), ((), ())),
                preferred_element_type=jnp.float32,
            )
            total = part if total is None else total + part
        for ref in add_refs:
            total = total + ref[...]
        out_ref[...] = total.astype(out_dtype)
        for fetch in fetches:
            fetch.wait()

    anywhere = pl.BlockSpec(memory_space=pltpu.HBM)
    vmem = pl.BlockSpec(memory_space=pltpu.VMEM)
    scratch = []
    if not ready:
        scratch += [pltpu.VMEM((features, w), jnp.bfloat16) for w in widths]
        scratch += [pltpu.SemaphoreType.DMA((count,))]
    if later:
        scratch += [pltpu.SemaphoreType.DMA((later,))]
    room = 2 * sum(widths) * (rows + features) + 2 * features * sum(u for _, u in ahead)
    room += 4 * rows * features * (1 + len(added))
    moved = sum(widths) * (rows + features) + features * sum(units for _, units in ahead)
    out = pl.pallas_call(
        body,
        out_shape=[jax.ShapeDtypeStruct((rows, features), out_dtype)]
        + [jax.ShapeDtypeStruct((features, units), jnp.bfloat16) for _, units in ahead],
        in_specs=[pl.BlockSpec(memory_space=pltpu.SMEM)]
        + [vmem] * count
        + [anywhere]
        + [vmem] * (len(ready) + len(added)),
        out_specs=[vmem] * (1 + later),
        scratch_shapes=scratch,
        cost_estimate=pl.CostEstimate(
            flops=2 * rows * sum(widths) * features,
            transcendentals=0,
            bytes_accessed=2 * moved + 8 * rows * features,
        ),
        compiler_params=pltpu.CompilerParams(vmem_limit_bytes=room + (5 << 20)),
    )(starts, *chunks, in_hbm(weight), *ready, *added)
    return out[0], out[1:]


def adapter_kernel(mine, other, core, labels, outputs):
    count, rank, width = outputs.shape
    part, cols = mine.shape
    total = 2 * part

    def body(core_ref, mine_ref, other_ref, l_ref, w_ref, o_ref, s_ref):
        at = core_ref[0]
        s_ref[pl.ds(pl.multiple_of(at * part, 8), part), :] = mine_ref[...]
        s_ref[pl.ds(pl.multiple_of((1 - at) * part, 8), part), :] = other_ref[...]
        summed = s_ref[...]
        label = l_ref[...]
        shrunk = jnp.where(label != 0, summed, 0.0).astype(jnp.bfloat16).astype(jnp.float32)
        own = shrunk[:, :rank]
        spread = jnp.concatenate([jnp.where(label == k, own, 0.0) for k in range(count)], axis=1)
        update = jnp.dot(
            spread.astype(jnp.bfloat16), w_ref[...], preferred_element_type=jnp.float32
        )
        resident = summed[:, rank:]
        high = resident.astype(jnp.bfloat16)
        left = resident - high.astype(jnp.float32)
        middle = left.astype(jnp.bfloat16)
        low = (left - middle.astype(jnp.float32)).astype(jnp.bfloat16)
        first = w_ref[:rank, :]
        taken = shrunk[:, rank:].astype(jnp.bfloat16)
        base = jnp.dot(low, first, preferred_element_type=jnp.float32)
        base = base + jnp.dot(middle, first, preferred_element_type=jnp.float32)
        base = base + jnp.dot(high, first, preferred_element_type=jnp.float32)
        o_ref[...] = base + (update - jnp.dot(taken, first, preferred_element_type=jnp.float32))

    vmem = pl.BlockSpec(memory_space=pltpu.VMEM)
    return pl.pallas_call(
        body,
        out_shape=jax.ShapeDtypeStruct((total, width), jnp.float32),
        in_specs=[pl.BlockSpec(memory_space=pltpu.SMEM)] + [vmem] * 4,
        out_specs=vmem,
        scratch_shapes=[pltpu.VMEM((total, cols), jnp.float32)],
        cost_estimate=pl.CostEstimate(
            flops=2 * total * (count + 4) * rank * width,
            transcendentals=0,
            bytes_accessed=2 * count * rank * width + 4 * total * (cols + width),
        ),
        compiler_params=pltpu.CompilerParams(vmem_limit_bytes=12 << 20),
    )(core.reshape(1), mine, other, labels[:, None], outputs.reshape(count * rank, width))


def solution(mesh):
    axis_size = mesh.shape["row"]
    ring, snake = chip_ring(mesh)
    chips, cores = len(ring), len(ring[0])
    turn_of = [1, -1]
    forward = [
        (ring[p][c], ring[(p + turn_of[c % 2]) % chips][c]) for p in range(chips) for c in range(cores)
    ]
    backward = [(b, a) for a, b in forward]
    partner = [(members[c], members[1 - c]) for members in ring for c in range(cores)] if cores == 2 else []

    long = chips // 2
    across = [(ring[p][c], ring[chips - 1 - p][c]) for p in range(chips) for c in range(cores)]
    lines = [
        [ring[p][c] for p in range(lo, lo + long)] for lo in (0, long) for c in range(cores)
    ]
    place = np.zeros((axis_size, 2), np.int32)
    for p, members in enumerate(ring):
        for c, at in enumerate(members):
            place[at] = c, int(p >= long)

    def plain(flat, weight, factors, outputs, labels):
        count, rank, units = factors.shape
        project_rows = jnp.dot(
            flat, factors.reshape(count * rank, units).T, preferred_element_type=jnp.float32
        )
        summed = sum_over_row(select_both(project_rows, labels, count, rank), axis_size)
        base = lax.dot_general(
            lax.all_gather(flat, "row", axis=1, tiled=True),
            weight,
            (((1,), (1,)), ((), ())),
            preferred_element_type=jnp.float32,
        )
        return (base + adapter_terms(summed, labels, outputs)).astype(jnp.bfloat16)

    def ringed(flat, weight, factors, outputs, labels):
        device_units = flat.shape[1]
        half = device_units // 2
        tiles = half // LANES
        cut = (tiles - tiles * 2 // 7) * LANES
        me = lax.axis_index("row")
        core, side = [jnp.asarray(place)[me][k] for k in range(2)]
        own = cut_block(flat, half)
        mine, other = project_selected(own, labels, factors, core)
        halves = sum_by_stages(mine, other, side, partner, across, lines)
        extra = adapter_kernel(*halves, core, labels, outputs)

        plan = [(s // 2 + 1, s % 2, 0, half) for s in range(2 * long - 2)]
        plan += [(long, 0, 0, cut), (long, 0, cut, half - cut)]
        beside = lax.ppermute(flat, "row", partner)
        batches = [[(own[part], 0, False, part, 0) for part in range(2)] + [(beside, 0, True, 0, 0)]]
        held = {"up": list(own), "down": list(own)}
        for distance, turn, column, width in plan:
            found = []
            for way, pairs, part in (("up", forward, turn), ("down", backward, 1 - turn)):
                send = held[way][part]
                if width < half:
                    send = send[:, column : column + width]
                data = lax.ppermute(send, "row", pairs)
                if width == half:
                    held[way][part] = data
                beside = lax.ppermute(data, "row", partner)
                offset = -distance if way == "up" else distance
                found.append((data, offset, False, part, column))
                found.append((beside, offset, True, part, column))
            batches.append(found)
        batches[-1:] = [batches[-1][::2], batches[-1][1::2]]
        order = [entry[1:] for found in batches for entry in found]
        table = np.zeros((axis_size, len(order)), np.int32)
        for p, members in enumerate(ring):
            for c, at in enumerate(members):
                for k, (offset, beside, part, column) in enumerate(order):
                    its = 1 - c if beside else c
                    source = ring[(p + offset * turn_of[its]) % chips][its]
                    table[at, k] = (source * device_units + part * half + column) // LANES
        starts = jnp.asarray(table)[me]
        acc, ready, done = [], [], 0
        ends = len(batches) - 2
        settled = min(3, ends - 2)
        for k, found in enumerate(batches):
            last = k == len(batches) - 1
            coming = []
            if settled <= k <= ends - 2:
                coming = batches[k + 1] if k < ends - 2 else sum(batches[k + 1 :], [])
            at = done + len(found)
            ahead = [(at + j, entry[0].shape[1]) for j, entry in enumerate(coming)]
            out, fetched = chunk_matmul(
                [entry[0] for entry in found],
                starts,
                done,
                weight,
                acc + ([extra] if k == ends - 2 else []),
                jnp.bfloat16 if last else jnp.float32,
                ready[: len(found)],
                ahead,
            )
            ready = ready[len(found) :] + list(fetched)
            acc = [out]
            done += len(found)
        return acc[0]

    def local(
        gated_hidden_rows,
        down_base_weight,
        adapter_input_factor,
        adapter_output_weight,
        request_adapter_index,
    ):
        steps, requests, device_units = gated_hidden_rows.shape
        total = steps * requests
        fits = device_units % (2 * LANES) == 0 and total % (32 * max(long, 1)) == 0
        run = ringed if snake and cores == 2 and long > 1 and fits else plain
        out = run(
            gated_hidden_rows.reshape(total, device_units),
            down_base_weight,
            adapter_input_factor,
            adapter_output_weight,
            request_adapter_index.reshape(total),
        )
        return out.reshape(steps, requests, out.shape[1])

    placed = (
        P(None, "groups", "row"),
        P("row", None),
        P(None, None, "row"),
        P(None, None, "row"),
        P(None, "groups"),
    )

    return jax.shard_map(
        local, mesh=mesh, in_specs=placed, out_specs=P(None, "groups", "row"), check_vma=False
    )
```

```python
import jax
import jax.numpy as jnp
import numpy as np
from jax import lax
from jax.experimental import pallas as pl
from jax.experimental.pallas import tpu as pltpu
from jax.sharding import PartitionSpec as P


LANES = 128


def chip_ring(mesh):
    line = mesh.devices.reshape(mesh.devices.shape[0], -1)[0]
    chips = {}
    for at, device in enumerate(line):
        place = tuple(getattr(device, "coords", (at, 0, 0)))
        chips.setdefault(place, []).append(at)
    places = list(chips)
    if len({len(c) for c in chips.values()}) != 1:
        return [[at] for at in range(len(line))], False
    used = [k for k in range(len(places[0])) if len({p[k] for p in places}) > 1]
    if len(used) == 2:
        sizes = [len({p[k] for p in places}) for k in used]
        if 2 in sizes and sizes[0] * sizes[1] == len(places):
            short = used[sizes.index(2)]
            long = used[0] if short == used[1] else used[1]
            low = min(p[short] for p in places)
            up = sorted((p for p in places if p[short] == low), key=lambda p: p[long])
            down = sorted((p for p in places if p[short] != low), key=lambda p: -p[long])
            places = up + down
            return [chips[p] for p in places], True
    return [chips[p] for p in places], False


def in_hbm(array):
    return pltpu.with_memory_space_constraint(array, pltpu.HBM)


def cut_block(block, half):
    def body(x_ref, a_ref, b_ref, sem):
        copies = [
            pltpu.make_async_copy(x_ref.at[:, pl.ds(k * half, half)], out, sem.at[k])
            for k, out in enumerate((a_ref, b_ref))
        ]
        for copy in copies:
            copy.start()
        for copy in copies:
            copy.wait()

    vmem = pl.BlockSpec(memory_space=pltpu.VMEM)
    shape = jax.ShapeDtypeStruct((block.shape[0], half), block.dtype)
    return pl.pallas_call(
        body,
        out_shape=(shape, shape),
        in_specs=[pl.BlockSpec(memory_space=pltpu.HBM)],
        out_specs=(vmem, vmem),
        scratch_shapes=[pltpu.SemaphoreType.DMA((2,))],
        compiler_params=pltpu.CompilerParams(vmem_limit_bytes=4 << 20),
    )(in_hbm(block))


def project_selected(rows, labels, factors, first):
    count, rank, units = factors.shape
    total = rows[0].shape[0]
    half = units // 2
    wide = count * rank
    part = total // 2

    def body(f_ref, low_ref, high_ref, l_ref, a_any, mine_ref, other_ref, s_ref, a_ref, sem):
        copy = pltpu.make_async_copy(a_any, a_ref, sem)
        copy.start()
        copy.wait()
        full = sum(
            lax.dot_general(
                x_ref[...],
                a_ref[:, k * half : (k + 1) * half],
                (((1,), (1,)), ((), ())),
                preferred_element_type=jnp.float32,
            )
            for k, x_ref in enumerate((low_ref, high_ref))
        )
        own = jnp.zeros((total, rank), jnp.float32)
        for k in range(count):
            own = own + jnp.where(l_ref[...] == k, full[:, k * rank : (k + 1) * rank], 0.0)
        s_ref[...] = jnp.concatenate([own, full[:, :rank]], axis=1)
        at = f_ref[0]
        mine_ref[...] = s_ref[pl.ds(pl.multiple_of(at * part, 8), part), :]
        other_ref[...] = s_ref[pl.ds(pl.multiple_of((1 - at) * part, 8), part), :]

    vmem = pl.BlockSpec(memory_space=pltpu.VMEM)
    anywhere = pl.BlockSpec(memory_space=pltpu.HBM)
    shape = jax.ShapeDtypeStruct((part, 2 * rank), jnp.float32)
    return pl.pallas_call(
        body,
        out_shape=(shape, shape),
        in_specs=[pl.BlockSpec(memory_space=pltpu.SMEM), vmem, vmem, vmem, anywhere],
        out_specs=(vmem, vmem),
        scratch_shapes=[
            pltpu.VMEM((total, 2 * rank), jnp.float32),
            pltpu.VMEM((wide, units), jnp.bfloat16),
            pltpu.SemaphoreType.DMA,
        ],
        cost_estimate=pl.CostEstimate(
            flops=2 * total * wide * units,
            transcendentals=0,
            bytes_accessed=2 * units * (total + wide) + 8 * total * rank,
        ),
        compiler_params=pltpu.CompilerParams(vmem_limit_bytes=12 << 20),
    )(first.reshape(1), *rows, labels[:, None], in_hbm(factors.reshape(wide, units)))


def labels_onehot(adapter_labels, count):
    return adapter_labels[:, None] == jnp.arange(count, dtype=jnp.int32)[None, :]


def select_both(project_rows, adapter_labels, count, rank):
    choose = labels_onehot(adapter_labels, count).astype(jnp.float32)
    total = project_rows.shape[0]
    own = jnp.sum(project_rows.reshape(total, count, rank) * choose[:, :, None], axis=1)
    return jnp.concatenate([own, project_rows[:, :rank]], axis=1)


def expand_factor(shrunk_rows, adapter_labels, adapter_output_weight):
    count, rank, width = adapter_output_weight.shape
    total = shrunk_rows.shape[0]
    choose = labels_onehot(adapter_labels, count).astype(jnp.float32)
    spread = (choose[:, :, None] * shrunk_rows[:, None, :rank].astype(jnp.float32)).reshape(
        total, count * rank
    )
    operand = jnp.concatenate([spread.astype(jnp.bfloat16), shrunk_rows[:, rank:]], axis=1)
    stacked = jnp.concatenate(
        [adapter_output_weight.reshape(count * rank, width), -adapter_output_weight[0]], axis=0
    )
    return jnp.dot(operand, stacked, preferred_element_type=jnp.float32)


def adapter_terms(summed, labels, outputs):
    rank = outputs.shape[1]
    keep = (labels != 0).astype(jnp.float32)[:, None]
    shrunk_rows = (summed * keep).astype(jnp.bfloat16)
    resident = jnp.dot(
        summed[:, rank:], outputs[0].astype(jnp.float32), precision=lax.Precision.HIGHEST
    )
    return resident + expand_factor(shrunk_rows, labels, outputs)


def sum_over_row(summand, axis_size):
    rows, cols = summand.shape
    if rows % axis_size:
        return lax.psum(summand, "row")
    parts = lax.all_to_all(summand, "row", 0, 0, tiled=True)
    mine = jnp.sum(parts.reshape(axis_size, rows // axis_size, cols), axis=0)
    spread = jnp.broadcast_to(mine[None], (axis_size,) + mine.shape).reshape(rows, cols)
    return lax.all_to_all(spread, "row", 0, 0, tiled=True)


def swap(rows, at, pairs):
    part = rows.shape[0] // 2
    low, high = rows[:part], rows[part:]
    got = lax.ppermute(jnp.where(at == 0, high, low), "row", pairs)
    return jnp.where(at == 0, low, high) + got


def join(part, at, pairs):
    got = lax.ppermute(part, "row", pairs)
    return jnp.concatenate([jnp.where(at == 0, part, got), jnp.where(at == 0, got, part)], axis=0)


def sum_by_stages(mine, other, side, partner, across, lines):
    got = lax.ppermute(other, "row", partner)
    rows = swap(mine + got, side, across)
    size = len(lines[0])
    piece = rows.shape[0] // size
    parts = lax.all_to_all(rows, "row", 0, 0, axis_index_groups=lines, tiled=True)
    total = jnp.sum(parts.reshape(size, piece, rows.shape[1]), axis=0)
    spread = jnp.broadcast_to(total[None], (size,) + total.shape).reshape(rows.shape)
    whole = lax.all_to_all(spread, "row", 0, 0, axis_index_groups=lines, tiled=True)
    half = join(whole, side, across)
    return half, lax.ppermute(half, "row", partner)


def chunk_matmul(chunks, starts, first, weight, added, out_dtype, ready, ahead):
    count = len(chunks)
    rows = chunks[0].shape[0]
    widths = [c.shape[1] for c in chunks]
    features = weight.shape[0]
    later = len(ahead)

    def body(starts_ref, *refs):
        x_refs, refs = refs[:count], refs[count:]
        w_any, refs = refs[0], refs[1:]
        w_refs, refs = refs[: len(ready)], refs[len(ready) :]
        add_refs, refs = refs[: len(added)], refs[len(added) :]
        out_ref, ahead_refs, refs = refs[0], refs[1 : 1 + later], refs[1 + later :]

        def block(at, units):
            start = pl.multiple_of(starts_ref[at] * LANES, LANES)
            return w_any.at[:, pl.ds(start, units)]

        copies = []
        if not ready:
            w_refs, w_sem = refs[:count], refs[count]
            for k in range(count):
                copy = pltpu.make_async_copy(block(first + k, widths[k]), w_refs[k], w_sem.at[k])
                copy.start()
                copies.append(copy)
        fetches = [
            pltpu.make_async_copy(block(at, units), ahead_refs[k], refs[-1].at[k])
            for k, (at, units) in enumerate(ahead)
        ]
        for fetch in fetches:
            fetch.start()
        total = None
        for k in range(count):
            if copies:
                copies[k].wait()
            part = lax.dot_general(
                x_refs[k][...],
                w_refs[k][...],
                (((1,), (1,)), ((), ())),
                preferred_element_type=jnp.float32,
            )
            total = part if total is None else total + part
        for ref in add_refs:
            total = total + ref[...]
        out_ref[...] = total.astype(out_dtype)
        for fetch in fetches:
            fetch.wait()

    anywhere = pl.BlockSpec(memory_space=pltpu.HBM)
    vmem = pl.BlockSpec(memory_space=pltpu.VMEM)
    scratch = []
    if not ready:
        scratch += [pltpu.VMEM((features, w), jnp.bfloat16) for w in widths]
        scratch += [pltpu.SemaphoreType.DMA((count,))]
    if later:
        scratch += [pltpu.SemaphoreType.DMA((later,))]
    room = 2 * sum(widths) * (rows + features) + 2 * features * sum(u for _, u in ahead)
    room += 4 * rows * features * (1 + len(added))
    moved = sum(widths) * (rows + features) + features * sum(units for _, units in ahead)
    out = pl.pallas_call(
        body,
        out_shape=[jax.ShapeDtypeStruct((rows, features), out_dtype)]
        + [jax.ShapeDtypeStruct((features, units), jnp.bfloat16) for _, units in ahead],
        in_specs=[pl.BlockSpec(memory_space=pltpu.SMEM)]
        + [vmem] * count
        + [anywhere]
        + [vmem] * (len(ready) + len(added)),
        out_specs=[vmem] * (1 + later),
        scratch_shapes=scratch,
        cost_estimate=pl.CostEstimate(
            flops=2 * rows * sum(widths) * features,
            transcendentals=0,
            bytes_accessed=2 * moved + 8 * rows * features,
        ),
        compiler_params=pltpu.CompilerParams(vmem_limit_bytes=room + (5 << 20)),
    )(starts, *chunks, in_hbm(weight), *ready, *added)
    return out[0], out[1:]


def row_cuts(total):
    unit = total // 24
    return [(0, 14 * unit), (14 * unit, 10 * unit)]


def rows_matmul(chunks, blocks, acc, row, out, final):
    count = len(chunks)
    rows = chunks[0].shape[0]
    features = blocks[0].shape[0]
    total = acc.shape[0] if out is None else out.shape[0]

    def body(*refs):
        x_refs, w_refs, a_ref, refs = refs[:count], refs[count : 2 * count], refs[2 * count], refs[2 * count + 1 :]
        value = a_ref[...] if a_ref.shape[0] == rows else a_ref[row : row + rows, :]
        for x_ref, w_ref in zip(x_refs, w_refs):
            value = value + lax.dot_general(
                x_ref[...], w_ref[...], (((1,), (1,)), ((), ())), preferred_element_type=jnp.float32
            )
        if final:
            o_ref, s_ref, sem = refs[-3:]
            s_ref[...] = value.astype(jnp.bfloat16)
            copy = pltpu.make_async_copy(s_ref, o_ref.at[pl.ds(row, rows)], sem)
            copy.start()
            copy.wait()
        else:
            refs[0][...] = value

    anywhere = pl.BlockSpec(memory_space=pltpu.HBM)
    vmem = pl.BlockSpec(memory_space=pltpu.VMEM)
    shape = jax.ShapeDtypeStruct((total, features), jnp.bfloat16)
    if not final:
        shape = jax.ShapeDtypeStruct((rows, features), jnp.float32)
    return pl.pallas_call(
        body,
        out_shape=shape,
        in_specs=[vmem] * (2 * count + 1) + ([] if out is None else [anywhere]),
        out_specs=anywhere if final else vmem,
        scratch_shapes=[pltpu.VMEM((rows, features), jnp.bfloat16), pltpu.SemaphoreType.DMA] if final else [],
        input_output_aliases={} if out is None else {2 * count + 1: 0},
        compiler_params=pltpu.CompilerParams(vmem_limit_bytes=16 << 20),
    )(*chunks, *blocks, acc, *([] if out is None else [out]))


def adapter_kernel(mine, other, core, labels, outputs):
    count, rank, width = outputs.shape
    part, cols = mine.shape
    total = 2 * part

    def body(core_ref, mine_ref, other_ref, l_ref, w_ref, o_ref, s_ref):
        at = core_ref[0]
        s_ref[pl.ds(pl.multiple_of(at * part, 8), part), :] = mine_ref[...]
        s_ref[pl.ds(pl.multiple_of((1 - at) * part, 8), part), :] = other_ref[...]
        summed = s_ref[...]
        label = l_ref[...]
        shrunk = jnp.where(label != 0, summed, 0.0).astype(jnp.bfloat16).astype(jnp.float32)
        own = shrunk[:, :rank]
        spread = jnp.concatenate([jnp.where(label == k, own, 0.0) for k in range(count)], axis=1)
        update = jnp.dot(
            spread.astype(jnp.bfloat16), w_ref[...], preferred_element_type=jnp.float32
        )
        resident = summed[:, rank:]
        high = resident.astype(jnp.bfloat16)
        left = resident - high.astype(jnp.float32)
        middle = left.astype(jnp.bfloat16)
        low = (left - middle.astype(jnp.float32)).astype(jnp.bfloat16)
        first = w_ref[:rank, :]
        taken = shrunk[:, rank:].astype(jnp.bfloat16)
        base = jnp.dot(low, first, preferred_element_type=jnp.float32)
        base = base + jnp.dot(middle, first, preferred_element_type=jnp.float32)
        base = base + jnp.dot(high, first, preferred_element_type=jnp.float32)
        o_ref[...] = base + (update - jnp.dot(taken, first, preferred_element_type=jnp.float32))

    vmem = pl.BlockSpec(memory_space=pltpu.VMEM)
    return pl.pallas_call(
        body,
        out_shape=jax.ShapeDtypeStruct((total, width), jnp.float32),
        in_specs=[pl.BlockSpec(memory_space=pltpu.SMEM)] + [vmem] * 4,
        out_specs=vmem,
        scratch_shapes=[pltpu.VMEM((total, cols), jnp.float32)],
        cost_estimate=pl.CostEstimate(
            flops=2 * total * (count + 4) * rank * width,
            transcendentals=0,
            bytes_accessed=2 * count * rank * width + 4 * total * (cols + width),
        ),
        compiler_params=pltpu.CompilerParams(vmem_limit_bytes=12 << 20),
    )(core.reshape(1), mine, other, labels[:, None], outputs.reshape(count * rank, width))


def solution(mesh):
    axis_size = mesh.shape["row"]
    ring, snake = chip_ring(mesh)
    chips, cores = len(ring), len(ring[0])
    turn_of = [1, -1]
    forward = [
        (ring[p][c], ring[(p + turn_of[c % 2]) % chips][c]) for p in range(chips) for c in range(cores)
    ]
    backward = [(b, a) for a, b in forward]
    partner = [(members[c], members[1 - c]) for members in ring for c in range(cores)] if cores == 2 else []

    long = chips // 2
    across = [(ring[p][c], ring[chips - 1 - p][c]) for p in range(chips) for c in range(cores)]
    lines = [
        [ring[p][c] for p in range(lo, lo + long)] for lo in (0, long) for c in range(cores)
    ]
    place = np.zeros((axis_size, 2), np.int32)
    for p, members in enumerate(ring):
        for c, at in enumerate(members):
            place[at] = c, int(p >= long)

    def plain(flat, weight, factors, outputs, labels):
        count, rank, units = factors.shape
        project_rows = jnp.dot(
            flat, factors.reshape(count * rank, units).T, preferred_element_type=jnp.float32
        )
        summed = sum_over_row(select_both(project_rows, labels, count, rank), axis_size)
        base = lax.dot_general(
            lax.all_gather(flat, "row", axis=1, tiled=True),
            weight,
            (((1,), (1,)), ((), ())),
            preferred_element_type=jnp.float32,
        )
        return (base + adapter_terms(summed, labels, outputs)).astype(jnp.bfloat16)

    def ringed(flat, weight, factors, outputs, labels):
        device_units = flat.shape[1]
        half = device_units // 2
        total = flat.shape[0]
        cuts = row_cuts(total)
        me = lax.axis_index("row")
        core, side = [jnp.asarray(place)[me][k] for k in range(2)]
        own = cut_block(flat, half)
        mine, other = project_selected(own, labels, factors, core)
        halves = sum_by_stages(mine, other, side, partner, across, lines)
        extra = adapter_kernel(*halves, core, labels, outputs)

        plan = [(s // 2 + 1, s % 2, 0, total) for s in range(2 * long - 2)]
        plan += [(long, 0, row, rows) for row, rows in cuts]
        beside = lax.ppermute(flat, "row", partner)
        batches = [[(own[part], 0, False, part) for part in range(2)] + [(beside, 0, True, 0)]]
        held = {"up": list(own), "down": list(own)}
        for distance, turn, row, rows in plan:
            found = []
            for way, pairs, part in (("up", forward, turn), ("down", backward, 1 - turn)):
                send = held[way][part]
                if rows < total:
                    send = send[row : row + rows]
                data = lax.ppermute(send, "row", pairs)
                if rows == total:
                    held[way][part] = data
                beside = lax.ppermute(data, "row", partner)
                offset = -distance if way == "up" else distance
                found.append((data, offset, False, part))
                found.append((beside, offset, True, part))
            batches.append(found)
        order = [entry[1:] for found in batches for entry in found]
        table = np.zeros((axis_size, len(order)), np.int32)
        for p, members in enumerate(ring):
            for c, at in enumerate(members):
                for k, (offset, beside, part) in enumerate(order):
                    its = 1 - c if beside else c
                    source = ring[(p + offset * turn_of[its]) % chips][its]
                    table[at, k] = (source * device_units + part * half) // LANES
        starts = jnp.asarray(table)[me]
        acc, ready, done = [], [], 0
        ends = len(batches) - len(cuts)
        settled = min(3, ends - 1)
        for k, found in enumerate(batches[:ends]):
            coming = batches[k + 1] if k >= settled else []
            at = done + len(found)
            ahead = [(at + j, half) for j, _ in enumerate(coming)]
            out, ready_next = chunk_matmul(
                [entry[0] for entry in found],
                starts,
                done,
                weight,
                acc + ([extra] if k == ends - 1 else []),
                jnp.float32,
                ready,
                ahead,
            )
            acc, ready, done = [out], list(ready_next), at
        out = None
        for k, ((row, _), found) in enumerate(zip(cuts, batches[ends:])):
            chunks = [entry[0] for entry in found]
            rest = acc[0]
            if k == len(cuts) - 1:
                rest = rows_matmul(chunks[::2], ready[::2], rest, row, None, False)
                chunks, ready = chunks[1::2], ready[1::2]
            out = rows_matmul(chunks, ready, rest, row, out, True)
        return out

    def local(
        gated_hidden_rows,
        down_base_weight,
        adapter_input_factor,
        adapter_output_weight,
        request_adapter_index,
    ):
        steps, requests, device_units = gated_hidden_rows.shape
        total = steps * requests
        fits = device_units % (2 * LANES) == 0 and total % 384 == 0 and total % (32 * max(long, 1)) == 0
        run = ringed if snake and cores == 2 and long > 1 and fits else plain
        out = run(
            gated_hidden_rows.reshape(total, device_units),
            down_base_weight,
            adapter_input_factor,
            adapter_output_weight,
            request_adapter_index.reshape(total),
        )
        return out.reshape(steps, requests, out.shape[1])

    placed = (
        P(None, "groups", "row"),
        P("row", None),
        P(None, None, "row"),
        P(None, None, "row"),
        P(None, "groups"),
    )

    return jax.shard_map(local, mesh=mesh, in_specs=placed, out_specs=P(None, "groups", "row"), check_vma=False)
```

```python
import jax
import jax.numpy as jnp
import numpy as np
from jax import lax
from jax.experimental import pallas as pl
from jax.experimental.pallas import tpu as pltpu
from jax.sharding import PartitionSpec as P


LANES = 128


def chip_ring(mesh):
    line = mesh.devices.reshape(mesh.devices.shape[0], -1)[0]
    chips = {}
    for at, device in enumerate(line):
        place = tuple(getattr(device, "coords", (at, 0, 0)))
        chips.setdefault(place, []).append(at)
    places = list(chips)
    if len({len(c) for c in chips.values()}) != 1:
        return [[at] for at in range(len(line))], False
    used = [k for k in range(len(places[0])) if len({p[k] for p in places}) > 1]
    if len(used) == 2:
        sizes = [len({p[k] for p in places}) for k in used]
        if 2 in sizes and sizes[0] * sizes[1] == len(places):
            short = used[sizes.index(2)]
            long = used[0] if short == used[1] else used[1]
            low = min(p[short] for p in places)
            up = sorted((p for p in places if p[short] == low), key=lambda p: p[long])
            down = sorted((p for p in places if p[short] != low), key=lambda p: -p[long])
            places = up + down
            return [chips[p] for p in places], True
    return [chips[p] for p in places], False


def in_hbm(array):
    return pltpu.with_memory_space_constraint(array, pltpu.HBM)


def cut_block(block, half):
    def body(x_ref, a_ref, b_ref, sem):
        copies = [
            pltpu.make_async_copy(x_ref.at[:, pl.ds(k * half, half)], out, sem.at[k])
            for k, out in enumerate((a_ref, b_ref))
        ]
        for copy in copies:
            copy.start()
        for copy in copies:
            copy.wait()

    vmem = pl.BlockSpec(memory_space=pltpu.VMEM)
    shape = jax.ShapeDtypeStruct((block.shape[0], half), block.dtype)
    return pl.pallas_call(
        body,
        out_shape=(shape, shape),
        in_specs=[pl.BlockSpec(memory_space=pltpu.HBM)],
        out_specs=(vmem, vmem),
        scratch_shapes=[pltpu.SemaphoreType.DMA((2,))],
        compiler_params=pltpu.CompilerParams(vmem_limit_bytes=4 << 20),
    )(in_hbm(block))


def project_selected(rows, labels, factors, first):
    count, rank, units = factors.shape
    total = rows[0].shape[0]
    half = units // 2
    wide = count * rank
    part = total // 2

    def body(f_ref, low_ref, high_ref, l_ref, a_any, mine_ref, other_ref, s_ref, a_ref, sem):
        copy = pltpu.make_async_copy(a_any, a_ref, sem)
        copy.start()
        copy.wait()
        full = sum(
            lax.dot_general(
                x_ref[...],
                a_ref[:, k * half : (k + 1) * half],
                (((1,), (1,)), ((), ())),
                preferred_element_type=jnp.float32,
            )
            for k, x_ref in enumerate((low_ref, high_ref))
        )
        own = jnp.zeros((total, rank), jnp.float32)
        for k in range(count):
            own = own + jnp.where(l_ref[...] == k, full[:, k * rank : (k + 1) * rank], 0.0)
        s_ref[...] = jnp.concatenate([own, full[:, :rank]], axis=1)
        at = f_ref[0]
        mine_ref[...] = s_ref[pl.ds(pl.multiple_of(at * part, 8), part), :]
        other_ref[...] = s_ref[pl.ds(pl.multiple_of((1 - at) * part, 8), part), :]

    vmem = pl.BlockSpec(memory_space=pltpu.VMEM)
    anywhere = pl.BlockSpec(memory_space=pltpu.HBM)
    shape = jax.ShapeDtypeStruct((part, 2 * rank), jnp.float32)
    return pl.pallas_call(
        body,
        out_shape=(shape, shape),
        in_specs=[pl.BlockSpec(memory_space=pltpu.SMEM), vmem, vmem, vmem, anywhere],
        out_specs=(vmem, vmem),
        scratch_shapes=[
            pltpu.VMEM((total, 2 * rank), jnp.float32),
            pltpu.VMEM((wide, units), jnp.bfloat16),
            pltpu.SemaphoreType.DMA,
        ],
        cost_estimate=pl.CostEstimate(
            flops=2 * total * wide * units,
            transcendentals=0,
            bytes_accessed=2 * units * (total + wide) + 8 * total * rank,
        ),
        compiler_params=pltpu.CompilerParams(vmem_limit_bytes=12 << 20),
    )(first.reshape(1), *rows, labels[:, None], in_hbm(factors.reshape(wide, units)))


def labels_onehot(adapter_labels, count):
    return adapter_labels[:, None] == jnp.arange(count, dtype=jnp.int32)[None, :]


def select_both(project_rows, adapter_labels, count, rank):
    choose = labels_onehot(adapter_labels, count).astype(jnp.float32)
    total = project_rows.shape[0]
    own = jnp.sum(project_rows.reshape(total, count, rank) * choose[:, :, None], axis=1)
    return jnp.concatenate([own, project_rows[:, :rank]], axis=1)


def expand_factor(shrunk_rows, adapter_labels, adapter_output_weight):
    count, rank, width = adapter_output_weight.shape
    total = shrunk_rows.shape[0]
    choose = labels_onehot(adapter_labels, count).astype(jnp.float32)
    spread = (choose[:, :, None] * shrunk_rows[:, None, :rank].astype(jnp.float32)).reshape(
        total, count * rank
    )
    operand = jnp.concatenate([spread.astype(jnp.bfloat16), shrunk_rows[:, rank:]], axis=1)
    stacked = jnp.concatenate(
        [adapter_output_weight.reshape(count * rank, width), -adapter_output_weight[0]], axis=0
    )
    return jnp.dot(operand, stacked, preferred_element_type=jnp.float32)


def adapter_terms(summed, labels, outputs):
    rank = outputs.shape[1]
    keep = (labels != 0).astype(jnp.float32)[:, None]
    shrunk_rows = (summed * keep).astype(jnp.bfloat16)
    resident = jnp.dot(
        summed[:, rank:], outputs[0].astype(jnp.float32), precision=lax.Precision.HIGHEST
    )
    return resident + expand_factor(shrunk_rows, labels, outputs)


def sum_over_row(summand, axis_size):
    rows, cols = summand.shape
    if rows % axis_size:
        return lax.psum(summand, "row")
    parts = lax.all_to_all(summand, "row", 0, 0, tiled=True)
    mine = jnp.sum(parts.reshape(axis_size, rows // axis_size, cols), axis=0)
    spread = jnp.broadcast_to(mine[None], (axis_size,) + mine.shape).reshape(rows, cols)
    return lax.all_to_all(spread, "row", 0, 0, tiled=True)


def swap(rows, at, pairs):
    part = rows.shape[0] // 2
    low, high = rows[:part], rows[part:]
    got = lax.ppermute(jnp.where(at == 0, high, low), "row", pairs)
    return jnp.where(at == 0, low, high) + got


def join(part, at, pairs):
    got = lax.ppermute(part, "row", pairs)
    return jnp.concatenate([jnp.where(at == 0, part, got), jnp.where(at == 0, got, part)], axis=0)


def rounded_pair(summed):
    rank = summed.shape[1] // 2
    resident = summed[:, rank:]
    left = resident - lax.reduce_precision(resident, exponent_bits=8, mantissa_bits=7)
    return jnp.concatenate([summed[:, :rank], left], axis=1).astype(jnp.bfloat16)


def sum_by_stages(mine, other, side, partner, across, lines):
    got = lax.ppermute(other, "row", partner)
    rows = swap(mine + got, side, across)
    size = len(lines[0])
    piece = rows.shape[0] // size
    parts = lax.all_to_all(rows, "row", 0, 0, axis_index_groups=lines, tiled=True)
    total = rounded_pair(jnp.sum(parts.reshape(size, piece, rows.shape[1]), axis=0))
    spread = jnp.broadcast_to(total[None], (size,) + total.shape).reshape(rows.shape)
    whole = lax.all_to_all(spread, "row", 0, 0, axis_index_groups=lines, tiled=True)
    half = join(whole, side, across)
    return half, lax.ppermute(half, "row", partner)


def chunk_matmul(chunks, starts, first, weight, added, out_dtype, ready, ahead):
    count = len(chunks)
    rows = chunks[0].shape[0]
    widths = [c.shape[1] for c in chunks]
    features = weight.shape[0]
    later = len(ahead)

    def body(starts_ref, *refs):
        x_refs, refs = refs[:count], refs[count:]
        w_any, refs = refs[0], refs[1:]
        w_refs, refs = refs[: len(ready)], refs[len(ready) :]
        add_refs, refs = refs[: len(added)], refs[len(added) :]
        out_ref, ahead_refs, refs = refs[0], refs[1 : 1 + later], refs[1 + later :]

        def block(at, units):
            start = pl.multiple_of(starts_ref[at] * LANES, LANES)
            return w_any.at[:, pl.ds(start, units)]

        copies = []
        if not ready:
            w_refs, w_sem = refs[:count], refs[count]
            for k in range(count):
                copy = pltpu.make_async_copy(block(first + k, widths[k]), w_refs[k], w_sem.at[k])
                copy.start()
                copies.append(copy)
        fetches = [
            pltpu.make_async_copy(block(at, units), ahead_refs[k], refs[-1].at[k])
            for k, (at, units) in enumerate(ahead)
        ]
        for fetch in fetches:
            fetch.start()
        total = None
        for k in range(count):
            if copies:
                copies[k].wait()
            part = lax.dot_general(
                x_refs[k][...],
                w_refs[k][...],
                (((1,), (1,)), ((), ())),
                preferred_element_type=jnp.float32,
            )
            total = part if total is None else total + part
        for ref in add_refs:
            total = total + ref[...]
        out_ref[...] = total.astype(out_dtype)
        for fetch in fetches:
            fetch.wait()

    anywhere = pl.BlockSpec(memory_space=pltpu.HBM)
    vmem = pl.BlockSpec(memory_space=pltpu.VMEM)
    scratch = []
    if not ready:
        scratch += [pltpu.VMEM((features, w), jnp.bfloat16) for w in widths]
        scratch += [pltpu.SemaphoreType.DMA((count,))]
    if later:
        scratch += [pltpu.SemaphoreType.DMA((later,))]
    room = 2 * sum(widths) * (rows + features) + 2 * features * sum(u for _, u in ahead)
    room += 4 * rows * features * (1 + len(added))
    moved = sum(widths) * (rows + features) + features * sum(units for _, units in ahead)
    out = pl.pallas_call(
        body,
        out_shape=[jax.ShapeDtypeStruct((rows, features), out_dtype)]
        + [jax.ShapeDtypeStruct((features, units), jnp.bfloat16) for _, units in ahead],
        in_specs=[pl.BlockSpec(memory_space=pltpu.SMEM)]
        + [vmem] * count
        + [anywhere]
        + [vmem] * (len(ready) + len(added)),
        out_specs=[vmem] * (1 + later),
        scratch_shapes=scratch,
        cost_estimate=pl.CostEstimate(
            flops=2 * rows * sum(widths) * features,
            transcendentals=0,
            bytes_accessed=2 * moved + 8 * rows * features,
        ),
        compiler_params=pltpu.CompilerParams(vmem_limit_bytes=room + (5 << 20)),
    )(starts, *chunks, in_hbm(weight), *ready, *added)
    return out[0], out[1:]


def row_cuts(total):
    unit = total // 24
    return [(0, 14 * unit), (14 * unit, 10 * unit)]


def rows_matmul(chunks, blocks, acc, row, out, final):
    count = len(chunks)
    rows = chunks[0].shape[0]
    features = blocks[0].shape[0]
    total = acc.shape[0] if out is None else out.shape[0]

    def body(*refs):
        x_refs, w_refs, a_ref, refs = refs[:count], refs[count : 2 * count], refs[2 * count], refs[2 * count + 1 :]
        value = a_ref[...] if a_ref.shape[0] == rows else a_ref[row : row + rows, :]
        for x_ref, w_ref in zip(x_refs, w_refs):
            value = value + lax.dot_general(
                x_ref[...], w_ref[...], (((1,), (1,)), ((), ())), preferred_element_type=jnp.float32
            )
        if final:
            o_ref, s_ref, sem = refs[-3:]
            s_ref[...] = value.astype(jnp.bfloat16)
            copy = pltpu.make_async_copy(s_ref, o_ref.at[pl.ds(row, rows)], sem)
            copy.start()
            copy.wait()
        else:
            refs[0][...] = value

    anywhere = pl.BlockSpec(memory_space=pltpu.HBM)
    vmem = pl.BlockSpec(memory_space=pltpu.VMEM)
    shape = jax.ShapeDtypeStruct((total, features), jnp.bfloat16)
    if not final:
        shape = jax.ShapeDtypeStruct((rows, features), jnp.float32)
    return pl.pallas_call(
        body,
        out_shape=shape,
        in_specs=[vmem] * (2 * count + 1) + ([] if out is None else [anywhere]),
        out_specs=anywhere if final else vmem,
        scratch_shapes=[pltpu.VMEM((rows, features), jnp.bfloat16), pltpu.SemaphoreType.DMA] if final else [],
        input_output_aliases={} if out is None else {2 * count + 1: 0},
        compiler_params=pltpu.CompilerParams(vmem_limit_bytes=16 << 20),
    )(*chunks, *blocks, acc, *([] if out is None else [out]))


def adapter_kernel(mine, other, core, labels, outputs):
    count, rank, width = outputs.shape
    part, cols = mine.shape
    total = 2 * part

    def body(core_ref, mine_ref, other_ref, l_ref, w_ref, o_ref, s_ref):
        at = core_ref[0]
        s_ref[pl.ds(pl.multiple_of(at * part, 16), part), :] = mine_ref[...]
        s_ref[pl.ds(pl.multiple_of((1 - at) * part, 16), part), :] = other_ref[...]
        pair = s_ref[...]
        label = l_ref[...]
        own = pair[:, :rank].astype(jnp.float32)
        spread = jnp.concatenate([jnp.where(label == k, own, 0.0) for k in range(count)], axis=1)
        update = jnp.dot(
            spread.astype(jnp.bfloat16), w_ref[...], preferred_element_type=jnp.float32
        )
        o_ref[...] = update + jnp.dot(
            pair[:, rank:], w_ref[:rank, :], preferred_element_type=jnp.float32
        )

    vmem = pl.BlockSpec(memory_space=pltpu.VMEM)
    return pl.pallas_call(
        body,
        out_shape=jax.ShapeDtypeStruct((total, width), jnp.float32),
        in_specs=[pl.BlockSpec(memory_space=pltpu.SMEM)] + [vmem] * 4,
        out_specs=vmem,
        scratch_shapes=[pltpu.VMEM((total, cols), jnp.bfloat16)],
        cost_estimate=pl.CostEstimate(
            flops=2 * total * (count + 1) * rank * width,
            transcendentals=0,
            bytes_accessed=2 * count * rank * width + 2 * total * cols + 4 * total * width,
        ),
        compiler_params=pltpu.CompilerParams(vmem_limit_bytes=12 << 20),
    )(core.reshape(1), mine, other, labels[:, None], outputs.reshape(count * rank, width))


def solution(mesh):
    axis_size = mesh.shape["row"]
    ring, snake = chip_ring(mesh)
    chips, cores = len(ring), len(ring[0])
    turn_of = [1, -1]
    forward = [
        (ring[p][c], ring[(p + turn_of[c % 2]) % chips][c]) for p in range(chips) for c in range(cores)
    ]
    backward = [(b, a) for a, b in forward]
    partner = [(members[c], members[1 - c]) for members in ring for c in range(cores)] if cores == 2 else []

    long = chips // 2
    across = [(ring[p][c], ring[chips - 1 - p][c]) for p in range(chips) for c in range(cores)]
    lines = [
        [ring[p][c] for p in range(lo, lo + long)] for lo in (0, long) for c in range(cores)
    ]
    place = np.zeros((axis_size, 2), np.int32)
    for p, members in enumerate(ring):
        for c, at in enumerate(members):
            place[at] = c, int(p >= long)

    def plain(flat, weight, factors, outputs, labels):
        count, rank, units = factors.shape
        project_rows = jnp.dot(
            flat, factors.reshape(count * rank, units).T, preferred_element_type=jnp.float32
        )
        summed = sum_over_row(select_both(project_rows, labels, count, rank), axis_size)
        base = lax.dot_general(
            lax.all_gather(flat, "row", axis=1, tiled=True),
            weight,
            (((1,), (1,)), ((), ())),
            preferred_element_type=jnp.float32,
        )
        return (base + adapter_terms(summed, labels, outputs)).astype(jnp.bfloat16)

    def ringed(flat, weight, factors, outputs, labels):
        device_units = flat.shape[1]
        half = device_units // 2
        total = flat.shape[0]
        cuts = row_cuts(total)
        me = lax.axis_index("row")
        core, side = [jnp.asarray(place)[me][k] for k in range(2)]
        own = cut_block(flat, half)
        mine, other = project_selected(own, labels, factors, core)
        halves = sum_by_stages(mine, other, side, partner, across, lines)
        extra = adapter_kernel(*halves, core, labels, outputs)

        plan = [(s // 2 + 1, s % 2, 0, total) for s in range(2 * long - 2)]
        plan += [(long, 0, row, rows) for row, rows in cuts]
        beside = lax.ppermute(flat, "row", partner)
        batches = [[(own[part], 0, False, part) for part in range(2)] + [(beside, 0, True, 0)]]
        held = {"up": list(own), "down": list(own)}
        for distance, turn, row, rows in plan:
            found = []
            for way, pairs, part in (("up", forward, turn), ("down", backward, 1 - turn)):
                send = held[way][part]
                if rows < total:
                    send = send[row : row + rows]
                data = lax.ppermute(send, "row", pairs)
                if rows == total:
                    held[way][part] = data
                beside = lax.ppermute(data, "row", partner)
                offset = -distance if way == "up" else distance
                found.append((data, offset, False, part))
                found.append((beside, offset, True, part))
            batches.append(found)
        order = [entry[1:] for found in batches for entry in found]
        table = np.zeros((axis_size, len(order)), np.int32)
        for p, members in enumerate(ring):
            for c, at in enumerate(members):
                for k, (offset, beside, part) in enumerate(order):
                    its = 1 - c if beside else c
                    source = ring[(p + offset * turn_of[its]) % chips][its]
                    table[at, k] = (source * device_units + part * half) // LANES
        starts = jnp.asarray(table)[me]
        acc, ready, done = [], [], 0
        ends = len(batches) - len(cuts)
        settled = min(3, ends - 1)
        for k, found in enumerate(batches[:ends]):
            coming = batches[k + 1] if k >= settled else []
            at = done + len(found)
            ahead = [(at + j, half) for j, _ in enumerate(coming)]
            out, ready_next = chunk_matmul(
                [entry[0] for entry in found],
                starts,
                done,
                weight,
                acc + ([extra] if k == ends - 1 else []),
                jnp.float32,
                ready,
                ahead,
            )
            acc, ready, done = [out], list(ready_next), at
        out = None
        for k, ((row, _), found) in enumerate(zip(cuts, batches[ends:])):
            chunks = [entry[0] for entry in found]
            rest = acc[0]
            if k == len(cuts) - 1:
                rest = rows_matmul(chunks[::2], ready[::2], rest, row, None, False)
                chunks, ready = chunks[1::2], ready[1::2]
            out = rows_matmul(chunks, ready, rest, row, out, True)
        return out

    def local(
        gated_hidden_rows,
        down_base_weight,
        adapter_input_factor,
        adapter_output_weight,
        request_adapter_index,
    ):
        steps, requests, device_units = gated_hidden_rows.shape
        total = steps * requests
        fits = device_units % (2 * LANES) == 0 and total % 384 == 0 and total % (32 * max(long, 1)) == 0
        run = ringed if snake and cores == 2 and long > 1 and fits else plain
        out = run(
            gated_hidden_rows.reshape(total, device_units),
            down_base_weight,
            adapter_input_factor,
            adapter_output_weight,
            request_adapter_index.reshape(total),
        )
        return out.reshape(steps, requests, out.shape[1])

    placed = (
        P(None, "groups", "row"),
        P("row", None),
        P(None, None, "row"),
        P(None, None, "row"),
        P(None, "groups"),
    )

    return jax.shard_map(local, mesh=mesh, in_specs=placed, out_specs=P(None, "groups", "row"), check_vma=False)
```

```python
import jax
import jax.numpy as jnp
import numpy as np
from jax import lax
from jax.experimental import pallas as pl
from jax.experimental.pallas import tpu as pltpu
from jax.sharding import PartitionSpec as P


LANES = 128


def chip_ring(mesh):
    line = mesh.devices.reshape(mesh.devices.shape[0], -1)[0]
    chips = {}
    for at, device in enumerate(line):
        place = tuple(getattr(device, "coords", (at, 0, 0)))
        chips.setdefault(place, []).append(at)
    places = list(chips)
    if len({len(c) for c in chips.values()}) != 1:
        return [[at] for at in range(len(line))], False
    used = [k for k in range(len(places[0])) if len({p[k] for p in places}) > 1]
    if len(used) == 2:
        sizes = [len({p[k] for p in places}) for k in used]
        if 2 in sizes and sizes[0] * sizes[1] == len(places):
            short = used[sizes.index(2)]
            long = used[0] if short == used[1] else used[1]
            low = min(p[short] for p in places)
            up = sorted((p for p in places if p[short] == low), key=lambda p: p[long])
            down = sorted((p for p in places if p[short] != low), key=lambda p: -p[long])
            places = up + down
            return [chips[p] for p in places], True
    return [chips[p] for p in places], False


def in_hbm(array):
    return pltpu.with_memory_space_constraint(array, pltpu.HBM)


def cut_block(block, half, near=False):
    def body(x_ref, a_ref, b_ref, sem):
        copies = [
            pltpu.make_async_copy(x_ref.at[:, pl.ds(k * half, half)], out, sem.at[k])
            for k, out in enumerate((a_ref, b_ref))
        ]
        for copy in copies:
            copy.start()
        for copy in copies:
            copy.wait()

    vmem = pl.BlockSpec(memory_space=pltpu.VMEM)
    shape = jax.ShapeDtypeStruct((block.shape[0], half), block.dtype)
    return pl.pallas_call(
        body,
        out_shape=(shape, shape),
        in_specs=[vmem if near else pl.BlockSpec(memory_space=pltpu.HBM)],
        out_specs=(vmem, vmem),
        scratch_shapes=[pltpu.SemaphoreType.DMA((2,))],
        compiler_params=pltpu.CompilerParams(vmem_limit_bytes=4 << 20),
    )(block if near else in_hbm(block))


def project_selected(rows, labels, factors, first):
    count, rank, units = factors.shape
    total = rows[0].shape[0]
    half = units // 2
    wide = count * rank
    part = total // 2

    def body(f_ref, low_ref, high_ref, l_ref, a_any, mine_ref, other_ref, s_ref, a_ref, sem):
        copy = pltpu.make_async_copy(a_any, a_ref, sem)
        copy.start()
        copy.wait()
        full = sum(
            lax.dot_general(
                x_ref[...],
                a_ref[:, k * half : (k + 1) * half],
                (((1,), (1,)), ((), ())),
                preferred_element_type=jnp.float32,
            )
            for k, x_ref in enumerate((low_ref, high_ref))
        )
        own = jnp.zeros((total, rank), jnp.float32)
        for k in range(count):
            own = own + jnp.where(l_ref[...] == k, full[:, k * rank : (k + 1) * rank], 0.0)
        s_ref[...] = jnp.concatenate([own, full[:, :rank]], axis=1)
        at = f_ref[0]
        mine_ref[...] = s_ref[pl.ds(pl.multiple_of(at * part, 8), part), :]
        other_ref[...] = s_ref[pl.ds(pl.multiple_of((1 - at) * part, 8), part), :]

    vmem = pl.BlockSpec(memory_space=pltpu.VMEM)
    anywhere = pl.BlockSpec(memory_space=pltpu.HBM)
    shape = jax.ShapeDtypeStruct((part, 2 * rank), jnp.float32)
    return pl.pallas_call(
        body,
        out_shape=(shape, shape),
        in_specs=[pl.BlockSpec(memory_space=pltpu.SMEM), vmem, vmem, vmem, anywhere],
        out_specs=(vmem, vmem),
        scratch_shapes=[
            pltpu.VMEM((total, 2 * rank), jnp.float32),
            pltpu.VMEM((wide, units), jnp.bfloat16),
            pltpu.SemaphoreType.DMA,
        ],
        cost_estimate=pl.CostEstimate(
            flops=2 * total * wide * units,
            transcendentals=0,
            bytes_accessed=2 * units * (total + wide) + 8 * total * rank,
        ),
        compiler_params=pltpu.CompilerParams(vmem_limit_bytes=12 << 20),
    )(first.reshape(1), *rows, labels[:, None], in_hbm(factors.reshape(wide, units)))


def labels_onehot(adapter_labels, count):
    return adapter_labels[:, None] == jnp.arange(count, dtype=jnp.int32)[None, :]


def select_both(project_rows, adapter_labels, count, rank):
    choose = labels_onehot(adapter_labels, count).astype(jnp.float32)
    total = project_rows.shape[0]
    own = jnp.sum(project_rows.reshape(total, count, rank) * choose[:, :, None], axis=1)
    return jnp.concatenate([own, project_rows[:, :rank]], axis=1)


def expand_factor(shrunk_rows, adapter_labels, adapter_output_weight):
    count, rank, width = adapter_output_weight.shape
    total = shrunk_rows.shape[0]
    choose = labels_onehot(adapter_labels, count).astype(jnp.float32)
    spread = (choose[:, :, None] * shrunk_rows[:, None, :rank].astype(jnp.float32)).reshape(
        total, count * rank
    )
    operand = jnp.concatenate([spread.astype(jnp.bfloat16), shrunk_rows[:, rank:]], axis=1)
    stacked = jnp.concatenate(
        [adapter_output_weight.reshape(count * rank, width), -adapter_output_weight[0]], axis=0
    )
    return jnp.dot(operand, stacked, preferred_element_type=jnp.float32)


def adapter_terms(summed, labels, outputs):
    rank = outputs.shape[1]
    keep = (labels != 0).astype(jnp.float32)[:, None]
    shrunk_rows = (summed * keep).astype(jnp.bfloat16)
    resident = jnp.dot(
        summed[:, rank:], outputs[0].astype(jnp.float32), precision=lax.Precision.HIGHEST
    )
    return resident + expand_factor(shrunk_rows, labels, outputs)


def sum_over_row(summand, axis_size):
    rows, cols = summand.shape
    if rows % axis_size:
        return lax.psum(summand, "row")
    parts = lax.all_to_all(summand, "row", 0, 0, tiled=True)
    mine = jnp.sum(parts.reshape(axis_size, rows // axis_size, cols), axis=0)
    spread = jnp.broadcast_to(mine[None], (axis_size,) + mine.shape).reshape(rows, cols)
    return lax.all_to_all(spread, "row", 0, 0, tiled=True)


def swap(rows, at, pairs):
    part = rows.shape[0] // 2
    low, high = rows[:part], rows[part:]
    got = lax.ppermute(jnp.where(at == 0, high, low), "row", pairs)
    return jnp.where(at == 0, low, high) + got


def join(part, at, pairs):
    got = lax.ppermute(part, "row", pairs)
    return jnp.concatenate([jnp.where(at == 0, part, got), jnp.where(at == 0, got, part)], axis=0)


def rounded_pair(summed):
    rank = summed.shape[1] // 2
    resident = summed[:, rank:]
    left = resident - lax.reduce_precision(resident, exponent_bits=8, mantissa_bits=7)
    return jnp.concatenate([summed[:, :rank], left], axis=1).astype(jnp.bfloat16)


def sum_by_stages(mine, other, side, partner, across, lines):
    got = lax.ppermute(other, "row", partner)
    rows = swap(mine + got, side, across)
    size = len(lines[0])
    piece = rows.shape[0] // size
    parts = lax.all_to_all(rows, "row", 0, 0, axis_index_groups=lines, tiled=True)
    total = rounded_pair(jnp.sum(parts.reshape(size, piece, rows.shape[1]), axis=0))
    spread = jnp.broadcast_to(total[None], (size,) + total.shape).reshape(rows.shape)
    whole = lax.all_to_all(spread, "row", 0, 0, axis_index_groups=lines, tiled=True)
    half = join(whole, side, across)
    return half, lax.ppermute(half, "row", partner)


def chunk_matmul(chunks, starts, first, weight, added, out_dtype, ready, ahead):
    count = len(chunks)
    rows = chunks[0].shape[0]
    widths = [c.shape[1] for c in chunks]
    features = weight.shape[0]
    later = len(ahead)

    def body(starts_ref, *refs):
        x_refs, refs = refs[:count], refs[count:]
        w_any, refs = refs[0], refs[1:]
        w_refs, refs = refs[: len(ready)], refs[len(ready) :]
        add_refs, refs = refs[: len(added)], refs[len(added) :]
        out_ref, ahead_refs, refs = refs[0], refs[1 : 1 + later], refs[1 + later :]

        def block(at, units):
            start = pl.multiple_of(starts_ref[at] * LANES, LANES)
            return w_any.at[:, pl.ds(start, units)]

        copies = []
        if not ready:
            w_refs, w_sem = refs[:count], refs[count]
            for k in range(count):
                copy = pltpu.make_async_copy(block(first + k, widths[k]), w_refs[k], w_sem.at[k])
                copy.start()
                copies.append(copy)
        fetches = [
            pltpu.make_async_copy(block(at, units), ahead_refs[k], refs[-1].at[k])
            for k, (at, units) in enumerate(ahead)
        ]
        for fetch in fetches:
            fetch.start()
        total = None
        for k in range(count):
            if copies:
                copies[k].wait()
            part = lax.dot_general(
                x_refs[k][...],
                w_refs[k][...],
                (((1,), (1,)), ((), ())),
                preferred_element_type=jnp.float32,
            )
            total = part if total is None else total + part
        for ref in add_refs:
            total = total + ref[...]
        out_ref[...] = total.astype(out_dtype)
        for fetch in fetches:
            fetch.wait()

    anywhere = pl.BlockSpec(memory_space=pltpu.HBM)
    vmem = pl.BlockSpec(memory_space=pltpu.VMEM)
    scratch = []
    if not ready:
        scratch += [pltpu.VMEM((features, w), jnp.bfloat16) for w in widths]
        scratch += [pltpu.SemaphoreType.DMA((count,))]
    if later:
        scratch += [pltpu.SemaphoreType.DMA((later,))]
    room = 2 * sum(widths) * (rows + features) + 2 * features * sum(u for _, u in ahead)
    room += 4 * rows * features * (1 + len(added))
    moved = sum(widths) * (rows + features) + features * sum(units for _, units in ahead)
    out = pl.pallas_call(
        body,
        out_shape=[jax.ShapeDtypeStruct((rows, features), out_dtype)]
        + [jax.ShapeDtypeStruct((features, units), jnp.bfloat16) for _, units in ahead],
        in_specs=[pl.BlockSpec(memory_space=pltpu.SMEM)]
        + [vmem] * count
        + [anywhere]
        + [vmem] * (len(ready) + len(added)),
        out_specs=[vmem] * (1 + later),
        scratch_shapes=scratch,
        cost_estimate=pl.CostEstimate(
            flops=2 * rows * sum(widths) * features,
            transcendentals=0,
            bytes_accessed=2 * moved + 8 * rows * features,
        ),
        compiler_params=pltpu.CompilerParams(vmem_limit_bytes=room + (5 << 20)),
    )(starts, *chunks, in_hbm(weight), *ready, *added)
    return out[0], out[1:]


def row_cuts(total):
    unit = total // 24
    return [(0, 12 * unit), (12 * unit, 12 * unit)]


def rows_matmul(chunks, blocks, acc, row, out, final):
    count = len(chunks)
    rows = chunks[0].shape[0]
    features = blocks[0].shape[0]
    total = acc.shape[0] if out is None else out.shape[0]

    def body(*refs):
        x_refs, w_refs, a_ref, refs = refs[:count], refs[count : 2 * count], refs[2 * count], refs[2 * count + 1 :]
        value = a_ref[...] if a_ref.shape[0] == rows else a_ref[row : row + rows, :]
        for x_ref, w_ref in zip(x_refs, w_refs):
            value = value + lax.dot_general(
                x_ref[...], w_ref[...], (((1,), (1,)), ((), ())), preferred_element_type=jnp.float32
            )
        if final:
            o_ref, s_ref, sem = refs[-3:]
            s_ref[...] = value.astype(jnp.bfloat16)
            copy = pltpu.make_async_copy(s_ref, o_ref.at[pl.ds(row, rows)], sem)
            copy.start()
            copy.wait()
        else:
            refs[0][...] = value

    anywhere = pl.BlockSpec(memory_space=pltpu.HBM)
    vmem = pl.BlockSpec(memory_space=pltpu.VMEM)
    shape = jax.ShapeDtypeStruct((total, features), jnp.bfloat16)
    if not final:
        shape = jax.ShapeDtypeStruct((rows, features), jnp.float32)
    return pl.pallas_call(
        body,
        out_shape=shape,
        in_specs=[vmem] * (2 * count + 1) + ([] if out is None else [anywhere]),
        out_specs=anywhere if final else vmem,
        scratch_shapes=[pltpu.VMEM((rows, features), jnp.bfloat16), pltpu.SemaphoreType.DMA] if final else [],
        input_output_aliases={} if out is None else {2 * count + 1: 0},
        compiler_params=pltpu.CompilerParams(vmem_limit_bytes=16 << 20),
    )(*chunks, *blocks, acc, *([] if out is None else [out]))


def adapter_kernel(mine, other, core, labels, outputs):
    count, rank, width = outputs.shape
    part, cols = mine.shape
    total = 2 * part

    def body(core_ref, mine_ref, other_ref, l_ref, w_ref, o_ref, s_ref):
        at = core_ref[0]
        s_ref[pl.ds(pl.multiple_of(at * part, 16), part), :] = mine_ref[...]
        s_ref[pl.ds(pl.multiple_of((1 - at) * part, 16), part), :] = other_ref[...]
        pair = s_ref[...]
        label = l_ref[...]
        own = pair[:, :rank].astype(jnp.float32)
        spread = jnp.concatenate([jnp.where(label == k, own, 0.0) for k in range(count)], axis=1)
        update = jnp.dot(
            spread.astype(jnp.bfloat16), w_ref[...], preferred_element_type=jnp.float32
        )
        o_ref[...] = update + jnp.dot(
            pair[:, rank:], w_ref[:rank, :], preferred_element_type=jnp.float32
        )

    vmem = pl.BlockSpec(memory_space=pltpu.VMEM)
    return pl.pallas_call(
        body,
        out_shape=jax.ShapeDtypeStruct((total, width), jnp.float32),
        in_specs=[pl.BlockSpec(memory_space=pltpu.SMEM)] + [vmem] * 4,
        out_specs=vmem,
        scratch_shapes=[pltpu.VMEM((total, cols), jnp.bfloat16)],
        cost_estimate=pl.CostEstimate(
            flops=2 * total * (count + 1) * rank * width,
            transcendentals=0,
            bytes_accessed=2 * count * rank * width + 2 * total * cols + 4 * total * width,
        ),
        compiler_params=pltpu.CompilerParams(vmem_limit_bytes=12 << 20),
    )(core.reshape(1), mine, other, labels[:, None], outputs.reshape(count * rank, width))


def solution(mesh):
    axis_size = mesh.shape["row"]
    ring, snake = chip_ring(mesh)
    chips, cores = len(ring), len(ring[0])
    turn_of = [1, -1]
    forward = [
        (ring[p][c], ring[(p + turn_of[c % 2]) % chips][c]) for p in range(chips) for c in range(cores)
    ]
    backward = [(b, a) for a, b in forward]
    partner = [(members[c], members[1 - c]) for members in ring for c in range(cores)] if cores == 2 else []

    long = chips // 2
    across = [(ring[p][c], ring[chips - 1 - p][c]) for p in range(chips) for c in range(cores)]
    lines = [
        [ring[p][c] for p in range(lo, lo + long)] for lo in (0, long) for c in range(cores)
    ]
    place = np.zeros((axis_size, 2), np.int32)
    for p, members in enumerate(ring):
        for c, at in enumerate(members):
            place[at] = c, int(p >= long)

    def plain(flat, weight, factors, outputs, labels):
        count, rank, units = factors.shape
        project_rows = jnp.dot(
            flat, factors.reshape(count * rank, units).T, preferred_element_type=jnp.float32
        )
        summed = sum_over_row(select_both(project_rows, labels, count, rank), axis_size)
        base = lax.dot_general(
            lax.all_gather(flat, "row", axis=1, tiled=True),
            weight,
            (((1,), (1,)), ((), ())),
            preferred_element_type=jnp.float32,
        )
        return (base + adapter_terms(summed, labels, outputs)).astype(jnp.bfloat16)

    def ringed(flat, weight, factors, outputs, labels):
        device_units = flat.shape[1]
        half = device_units // 2
        total = flat.shape[0]
        cuts = row_cuts(total)
        me = lax.axis_index("row")
        core, side = [jnp.asarray(place)[me][k] for k in range(2)]
        own = cut_block(flat, half)
        mine, other = project_selected(own, labels, factors, core)
        halves = sum_by_stages(mine, other, side, partner, across, lines)
        extra = adapter_kernel(*halves, core, labels, outputs)

        beside = lax.ppermute(flat, "row", partner)
        batches = [[(own[part], 0, False, part) for part in range(2)] + [(beside, 0, True, 0)]]

        def hop(data, pairs, offset, part):
            data = lax.ppermute(data, "row", pairs)
            beside = lax.ppermute(data, "row", partner)
            return data, [(data, offset, False, part), (beside, offset, True, part)]

        block, whole = hop(flat, forward, -1, 0)
        ups = list(cut_block(block, half, True))
        downs = list(own)
        for s in range(2 * long - 2):
            distance, turn = s // 2 + 1, s % 2
            downs[1 - turn], found = hop(downs[1 - turn], backward, distance, 1 - turn)
            if s == 1:
                found = whole + found
            elif s > 1:
                ups[turn], more = hop(ups[turn], forward, -distance, turn)
                found = more + found
            batches.append(found)
        for row, rows in cuts:
            _, found = hop(ups[0][row : row + rows], forward, -long, 0)
            batches.append(found + hop(downs[1][row : row + rows], backward, long, 1)[1])
        order = [entry[1:] for found in batches for entry in found]
        table = np.zeros((axis_size, len(order)), np.int32)
        for p, members in enumerate(ring):
            for c, at in enumerate(members):
                for k, (offset, beside, part) in enumerate(order):
                    its = 1 - c if beside else c
                    source = ring[(p + offset * turn_of[its]) % chips][its]
                    table[at, k] = (source * device_units + part * half) // LANES
        starts = jnp.asarray(table)[me]
        acc, ready, done = [], [], 0
        ends = len(batches) - len(cuts)
        settled = min(4, ends - 1)
        for k, found in enumerate(batches[:ends]):
            coming = batches[k + 1] if k >= settled else []
            at = done + len(found)
            ahead = [(at + j, min(entry[0].shape[1], device_units)) for j, entry in enumerate(coming)]
            out, ready_next = chunk_matmul(
                [entry[0] for entry in found],
                starts,
                done,
                weight,
                acc + ([extra] if k == ends - 1 else []),
                jnp.float32,
                ready,
                ahead,
            )
            acc, ready, done = [out], list(ready_next), at
        out = None
        for k, ((row, _), found) in enumerate(zip(cuts, batches[ends:])):
            chunks = [entry[0] for entry in found]
            rest = acc[0]
            if k == len(cuts) - 1:
                rest = rows_matmul(chunks[::2], ready[::2], rest, row, None, False)
                chunks, ready = chunks[1::2], ready[1::2]
            out = rows_matmul(chunks, ready, rest, row, out, True)
        return out

    def local(
        gated_hidden_rows,
        down_base_weight,
        adapter_input_factor,
        adapter_output_weight,
        request_adapter_index,
    ):
        steps, requests, device_units = gated_hidden_rows.shape
        total = steps * requests
        fits = device_units % (2 * LANES) == 0 and total % 384 == 0 and total % (32 * max(long, 1)) == 0
        run = ringed if snake and cores == 2 and long > 1 and fits else plain
        out = run(
            gated_hidden_rows.reshape(total, device_units),
            down_base_weight,
            adapter_input_factor,
            adapter_output_weight,
            request_adapter_index.reshape(total),
        )
        return out.reshape(steps, requests, out.shape[1])

    placed = (
        P(None, "groups", "row"),
        P("row", None),
        P(None, None, "row"),
        P(None, None, "row"),
        P(None, "groups"),
    )


    return jax.shard_map(local, mesh=mesh, in_specs=placed, out_specs=P(None, "groups", "row"), check_vma=False)
```

```python
import jax
import jax.numpy as jnp
import numpy as np
from jax import lax
from jax.experimental import pallas as pl
from jax.experimental.pallas import tpu as pltpu
from jax.sharding import PartitionSpec as P


LANES = 128
FAR = (0, 1, 2, 3, 4)


def chip_ring(mesh):
    line = mesh.devices.reshape(mesh.devices.shape[0], -1)[0]
    chips = {}
    for at, device in enumerate(line):
        place = tuple(getattr(device, "coords", (at, 0, 0)))
        chips.setdefault(place, []).append(at)
    places = list(chips)
    if len({len(c) for c in chips.values()}) != 1:
        return [[at] for at in range(len(line))], False
    used = [k for k in range(len(places[0])) if len({p[k] for p in places}) > 1]
    if len(used) == 2:
        sizes = [len({p[k] for p in places}) for k in used]
        if 2 in sizes and sizes[0] * sizes[1] == len(places):
            short = used[sizes.index(2)]
            long = used[0] if short == used[1] else used[1]
            low = min(p[short] for p in places)
            up = sorted((p for p in places if p[short] == low), key=lambda p: p[long])
            down = sorted((p for p in places if p[short] != low), key=lambda p: -p[long])
            places = up + down
            return [chips[p] for p in places], True
    return [chips[p] for p in places], False


def in_hbm(array):
    return pltpu.with_memory_space_constraint(array, pltpu.HBM)


def cut_block(block, half, near=False):
    def body(x_ref, a_ref, b_ref, sem):
        copies = [
            pltpu.make_async_copy(x_ref.at[:, pl.ds(k * half, half)], out, sem.at[k])
            for k, out in enumerate((a_ref, b_ref))
        ]
        for copy in copies:
            copy.start()
        for copy in copies:
            copy.wait()

    vmem = pl.BlockSpec(memory_space=pltpu.VMEM)
    shape = jax.ShapeDtypeStruct((block.shape[0], half), block.dtype)
    return pl.pallas_call(
        body,
        out_shape=(shape, shape),
        in_specs=[vmem if near else pl.BlockSpec(memory_space=pltpu.HBM)],
        out_specs=(vmem, vmem),
        scratch_shapes=[pltpu.SemaphoreType.DMA((2,))],
        compiler_params=pltpu.CompilerParams(vmem_limit_bytes=4 << 20),
    )(block if near else in_hbm(block))


def project_selected(rows, labels, factors, first):
    count, rank, units = factors.shape
    total = rows[0].shape[0]
    half = units // 2
    wide = count * rank
    part = total // 2

    def body(f_ref, low_ref, high_ref, l_ref, a_any, mine_ref, other_ref, s_ref, a_ref, sem):
        copy = pltpu.make_async_copy(a_any, a_ref, sem)
        copy.start()
        copy.wait()
        full = sum(
            lax.dot_general(
                x_ref[...],
                a_ref[:, k * half : (k + 1) * half],
                (((1,), (1,)), ((), ())),
                preferred_element_type=jnp.float32,
            )
            for k, x_ref in enumerate((low_ref, high_ref))
        )
        own = jnp.zeros((total, rank), jnp.float32)
        for k in range(count):
            own = own + jnp.where(l_ref[...] == k, full[:, k * rank : (k + 1) * rank], 0.0)
        s_ref[...] = jnp.concatenate([own, full[:, :rank]], axis=1)
        at = f_ref[0]
        mine_ref[...] = s_ref[pl.ds(pl.multiple_of(at * part, 8), part), :]
        other_ref[...] = s_ref[pl.ds(pl.multiple_of((1 - at) * part, 8), part), :]

    vmem = pl.BlockSpec(memory_space=pltpu.VMEM)
    anywhere = pl.BlockSpec(memory_space=pltpu.HBM)
    shape = jax.ShapeDtypeStruct((part, 2 * rank), jnp.float32)
    return pl.pallas_call(
        body,
        out_shape=(shape, shape),
        in_specs=[pl.BlockSpec(memory_space=pltpu.SMEM), vmem, vmem, vmem, anywhere],
        out_specs=(vmem, vmem),
        scratch_shapes=[
            pltpu.VMEM((total, 2 * rank), jnp.float32),
            pltpu.VMEM((wide, units), jnp.bfloat16),
            pltpu.SemaphoreType.DMA,
        ],
        cost_estimate=pl.CostEstimate(
            flops=2 * total * wide * units,
            transcendentals=0,
            bytes_accessed=2 * units * (total + wide) + 8 * total * rank,
        ),
        compiler_params=pltpu.CompilerParams(vmem_limit_bytes=12 << 20),
    )(first.reshape(1), *rows, labels[:, None], in_hbm(factors.reshape(wide, units)))


def labels_onehot(adapter_labels, count):
    return adapter_labels[:, None] == jnp.arange(count, dtype=jnp.int32)[None, :]


def select_both(project_rows, adapter_labels, count, rank):
    choose = labels_onehot(adapter_labels, count).astype(jnp.float32)
    total = project_rows.shape[0]
    own = jnp.sum(project_rows.reshape(total, count, rank) * choose[:, :, None], axis=1)
    return jnp.concatenate([own, project_rows[:, :rank]], axis=1)


def expand_factor(shrunk_rows, adapter_labels, adapter_output_weight):
    count, rank, width = adapter_output_weight.shape
    total = shrunk_rows.shape[0]
    choose = labels_onehot(adapter_labels, count).astype(jnp.float32)
    spread = (choose[:, :, None] * shrunk_rows[:, None, :rank].astype(jnp.float32)).reshape(
        total, count * rank
    )
    operand = jnp.concatenate([spread.astype(jnp.bfloat16), shrunk_rows[:, rank:]], axis=1)
    stacked = jnp.concatenate(
        [adapter_output_weight.reshape(count * rank, width), -adapter_output_weight[0]], axis=0
    )
    return jnp.dot(operand, stacked, preferred_element_type=jnp.float32)


def adapter_terms(summed, labels, outputs):
    rank = outputs.shape[1]
    keep = (labels != 0).astype(jnp.float32)[:, None]
    shrunk_rows = (summed * keep).astype(jnp.bfloat16)
    resident = jnp.dot(
        summed[:, rank:], outputs[0].astype(jnp.float32), precision=lax.Precision.HIGHEST
    )
    return resident + expand_factor(shrunk_rows, labels, outputs)


def sum_over_row(summand, axis_size):
    rows, cols = summand.shape
    if rows % axis_size:
        return lax.psum(summand, "row")
    parts = lax.all_to_all(summand, "row", 0, 0, tiled=True)
    mine = jnp.sum(parts.reshape(axis_size, rows // axis_size, cols), axis=0)
    spread = jnp.broadcast_to(mine[None], (axis_size,) + mine.shape).reshape(rows, cols)
    return lax.all_to_all(spread, "row", 0, 0, tiled=True)


def swap(rows, at, pairs):
    part = rows.shape[0] // 2
    low, high = rows[:part], rows[part:]
    got = lax.ppermute(jnp.where(at == 0, high, low), "row", pairs)
    return jnp.where(at == 0, low, high) + got


def join(part, at, pairs):
    got = lax.ppermute(part, "row", pairs)
    return jnp.concatenate([jnp.where(at == 0, part, got), jnp.where(at == 0, got, part)], axis=0)


def rounded_pair(summed):
    rank = summed.shape[1] // 2
    resident = summed[:, rank:]
    left = resident - lax.reduce_precision(resident, exponent_bits=8, mantissa_bits=7)
    return jnp.concatenate([summed[:, :rank], left], axis=1).astype(jnp.bfloat16)


def sum_by_stages(mine, other, side, partner, across, lines):
    got = lax.ppermute(other, "row", partner)
    rows = swap(mine + got, side, across)
    size = len(lines[0])
    piece = rows.shape[0] // size
    parts = lax.all_to_all(rows, "row", 0, 0, axis_index_groups=lines, tiled=True)
    total = rounded_pair(jnp.sum(parts.reshape(size, piece, rows.shape[1]), axis=0))
    spread = jnp.broadcast_to(total[None], (size,) + total.shape).reshape(rows.shape)
    whole = lax.all_to_all(spread, "row", 0, 0, axis_index_groups=lines, tiled=True)
    half = join(whole, side, across)
    return half, lax.ppermute(half, "row", partner)


def chunk_matmul(chunks, starts, first, weight, added, out_dtype, ready, ahead, far=False):
    count = len(chunks)
    rows = chunks[0].shape[0]
    widths = [c.shape[1] for c in chunks]
    features = weight.shape[0]
    later = len(ahead)

    def body(starts_ref, *refs):
        x_refs, refs = refs[:count], refs[count:]
        w_any, refs = refs[0], refs[1:]
        w_refs, refs = refs[: len(ready)], refs[len(ready) :]
        add_refs, refs = refs[: len(added)], refs[len(added) :]
        out_ref, ahead_refs, refs = refs[0], refs[1 : 1 + later], refs[1 + later :]

        def block(at, units):
            start = pl.multiple_of(starts_ref[at] * LANES, LANES)
            return w_any.at[:, pl.ds(start, units)]

        copies = []
        if far:
            near, x_sem, refs = refs[:count], refs[count], refs[count + 1 :]
            arrivals = [pltpu.make_async_copy(x_refs[k], near[k], x_sem.at[k]) for k in range(count)]
            for copy in arrivals:
                copy.start()
            x_refs = near
        if not ready:
            w_refs, w_sem = refs[:count], refs[count]
            for k in range(count):
                copy = pltpu.make_async_copy(block(first + k, widths[k]), w_refs[k], w_sem.at[k])
                copy.start()
                copies.append(copy)
        fetches = [
            pltpu.make_async_copy(block(at, units), ahead_refs[k], refs[-1].at[k])
            for k, (at, units) in enumerate(ahead)
        ]
        for fetch in fetches:
            fetch.start()
        total = None
        for k in range(count):
            if far:
                arrivals[k].wait()
            if copies:
                copies[k].wait()
            part = lax.dot_general(
                x_refs[k][...],
                w_refs[k][...],
                (((1,), (1,)), ((), ())),
                preferred_element_type=jnp.float32,
            )
            total = part if total is None else total + part
        for ref in add_refs:
            total = total + ref[...]
        out_ref[...] = total.astype(out_dtype)
        for fetch in fetches:
            fetch.wait()

    anywhere = pl.BlockSpec(memory_space=pltpu.HBM)
    vmem = pl.BlockSpec(memory_space=pltpu.VMEM)
    scratch = []
    if far:
        chunks = [in_hbm(chunk) for chunk in chunks]
        scratch += [pltpu.VMEM((rows, w), jnp.bfloat16) for w in widths]
        scratch += [pltpu.SemaphoreType.DMA((count,))]
    if not ready:
        scratch += [pltpu.VMEM((features, w), jnp.bfloat16) for w in widths]
        scratch += [pltpu.SemaphoreType.DMA((count,))]
    if later:
        scratch += [pltpu.SemaphoreType.DMA((later,))]
    room = 2 * sum(widths) * (rows + features) + 2 * features * sum(u for _, u in ahead)
    room += 4 * rows * features * (1 + len(added))
    moved = sum(widths) * (rows + features) + features * sum(units for _, units in ahead)
    out = pl.pallas_call(
        body,
        out_shape=[jax.ShapeDtypeStruct((rows, features), out_dtype)]
        + [jax.ShapeDtypeStruct((features, units), jnp.bfloat16) for _, units in ahead],
        in_specs=[pl.BlockSpec(memory_space=pltpu.SMEM)]
        + [anywhere if far else vmem] * count
        + [anywhere]
        + [vmem] * (len(ready) + len(added)),
        out_specs=[vmem] * (1 + later),
        scratch_shapes=scratch,
        cost_estimate=pl.CostEstimate(
            flops=2 * rows * sum(widths) * features,
            transcendentals=0,
            bytes_accessed=2 * moved + 8 * rows * features,
        ),
        compiler_params=pltpu.CompilerParams(vmem_limit_bytes=room + (5 << 20)),
    )(starts, *chunks, in_hbm(weight), *ready, *added)
    return out[0], out[1:]


def row_cuts(total):
    unit = total // 24
    return [(0, 12 * unit), (12 * unit, 12 * unit)]


def rows_matmul(chunks, blocks, acc, row, out, final):
    count = len(chunks)
    rows = chunks[0].shape[0]
    features = blocks[0].shape[0]
    total = acc.shape[0] if out is None else out.shape[0]

    def body(*refs):
        x_refs, w_refs, a_ref, refs = refs[:count], refs[count : 2 * count], refs[2 * count], refs[2 * count + 1 :]
        first = 0 if a_ref.shape[0] == rows else row
        pieces = 2 if final else 1
        wide = features // pieces
        copies = []
        for j in range(pieces):
            columns = pl.ds(j * wide, wide)
            value = a_ref[first : first + rows, j * wide : (j + 1) * wide]
            for x_ref, w_ref in zip(x_refs, w_refs):
                value = value + lax.dot_general(
                    x_ref[...],
                    w_ref[columns, :],
                    (((1,), (1,)), ((), ())),
                    preferred_element_type=jnp.float32,
                )
            if final:
                o_ref, s_ref, sem = refs[-3:]
                s_ref[:, columns] = value.astype(jnp.bfloat16)
                copies.append(
                    pltpu.make_async_copy(
                        s_ref.at[:, columns], o_ref.at[pl.ds(row, rows), columns], sem.at[j]
                    )
                )
                copies[-1].start()
            else:
                refs[0][...] = value
        for copy in copies:
            copy.wait()

    anywhere = pl.BlockSpec(memory_space=pltpu.HBM)
    vmem = pl.BlockSpec(memory_space=pltpu.VMEM)
    shape = jax.ShapeDtypeStruct((total, features), jnp.bfloat16)
    if not final:
        shape = jax.ShapeDtypeStruct((rows, features), jnp.float32)
    return pl.pallas_call(
        body,
        out_shape=shape,
        in_specs=[vmem] * (2 * count + 1) + ([] if out is None else [anywhere]),
        out_specs=anywhere if final else vmem,
        scratch_shapes=[pltpu.VMEM((rows, features), jnp.bfloat16), pltpu.SemaphoreType.DMA((2,))] if final else [],
        input_output_aliases={} if out is None else {2 * count + 1: 0},
        compiler_params=pltpu.CompilerParams(vmem_limit_bytes=16 << 20),
    )(*chunks, *blocks, acc, *([] if out is None else [out]))


def adapter_kernel(mine, other, core, labels, outputs):
    count, rank, width = outputs.shape
    part, cols = mine.shape
    total = 2 * part

    def body(core_ref, mine_ref, other_ref, l_ref, w_ref, o_ref, s_ref):
        at = core_ref[0]
        s_ref[pl.ds(pl.multiple_of(at * part, 16), part), :] = mine_ref[...]
        s_ref[pl.ds(pl.multiple_of((1 - at) * part, 16), part), :] = other_ref[...]
        pair = s_ref[...]
        label = l_ref[...]
        own = pair[:, :rank].astype(jnp.float32)
        spread = jnp.concatenate([jnp.where(label == k, own, 0.0) for k in range(count)], axis=1)
        update = jnp.dot(
            spread.astype(jnp.bfloat16), w_ref[...], preferred_element_type=jnp.float32
        )
        o_ref[...] = update + jnp.dot(
            pair[:, rank:], w_ref[:rank, :], preferred_element_type=jnp.float32
        )

    vmem = pl.BlockSpec(memory_space=pltpu.VMEM)
    return pl.pallas_call(
        body,
        out_shape=jax.ShapeDtypeStruct((total, width), jnp.float32),
        in_specs=[pl.BlockSpec(memory_space=pltpu.SMEM)] + [vmem] * 4,
        out_specs=vmem,
        scratch_shapes=[pltpu.VMEM((total, cols), jnp.bfloat16)],
        cost_estimate=pl.CostEstimate(
            flops=2 * total * (count + 1) * rank * width,
            transcendentals=0,
            bytes_accessed=2 * count * rank * width + 2 * total * cols + 4 * total * width,
        ),
        compiler_params=pltpu.CompilerParams(vmem_limit_bytes=12 << 20),
    )(core.reshape(1), mine, other, labels[:, None], outputs.reshape(count * rank, width))


def solution(mesh):
    axis_size = mesh.shape["row"]
    ring, snake = chip_ring(mesh)
    chips, cores = len(ring), len(ring[0])
    turn_of = [1, -1]
    forward = [
        (ring[p][c], ring[(p + turn_of[c % 2]) % chips][c]) for p in range(chips) for c in range(cores)
    ]
    backward = [(b, a) for a, b in forward]
    partner = [(members[c], members[1 - c]) for members in ring for c in range(cores)] if cores == 2 else []

    long = chips // 2
    across = [(ring[p][c], ring[chips - 1 - p][c]) for p in range(chips) for c in range(cores)]
    lines = [
        [ring[p][c] for p in range(lo, lo + long)] for lo in (0, long) for c in range(cores)
    ]
    place = np.zeros((axis_size, 2), np.int32)
    for p, members in enumerate(ring):
        for c, at in enumerate(members):
            place[at] = c, int(p >= long)

    def plain(flat, weight, factors, outputs, labels):
        count, rank, units = factors.shape
        project_rows = jnp.dot(
            flat, factors.reshape(count * rank, units).T, preferred_element_type=jnp.float32
        )
        summed = sum_over_row(select_both(project_rows, labels, count, rank), axis_size)
        base = lax.dot_general(
            lax.all_gather(flat, "row", axis=1, tiled=True),
            weight,
            (((1,), (1,)), ((), ())),
            preferred_element_type=jnp.float32,
        )
        return (base + adapter_terms(summed, labels, outputs)).astype(jnp.bfloat16)

    def ringed(flat, weight, factors, outputs, labels):
        device_units = flat.shape[1]
        half = device_units // 2
        total = flat.shape[0]
        cuts = row_cuts(total)
        me = lax.axis_index("row")
        core, side = [jnp.asarray(place)[me][k] for k in range(2)]
        own = cut_block(flat, half)
        mine, other = project_selected(own, labels, factors, core)
        halves = sum_by_stages(mine, other, side, partner, across, lines)
        extra = adapter_kernel(*halves, core, labels, outputs)

        beside = lax.ppermute(flat, "row", partner)
        batches = [[(own[part], 0, False, part) for part in range(2)] + [(beside, 0, True, 0)]]

        def hop(data, pairs, offset, part):
            data = lax.ppermute(data, "row", pairs)
            beside = lax.ppermute(data, "row", partner)
            return data, [(data, offset, False, part), (beside, offset, True, part)]

        block, whole = hop(flat, forward, -1, 0)
        ups = list(cut_block(block, half, True))
        downs = list(own)
        for s in range(2 * long - 2):
            distance, turn = s // 2 + 1, s % 2
            downs[1 - turn], found = hop(downs[1 - turn], backward, distance, 1 - turn)
            if s == 1:
                found = whole + found
            elif s > 1:
                ups[turn], more = hop(ups[turn], forward, -distance, turn)
                found = more + found
            batches.append(found)
        for row, rows in cuts:
            _, found = hop(ups[0][row : row + rows], forward, -long, 0)
            batches.append(found + hop(downs[1][row : row + rows], backward, long, 1)[1])
        order = [entry[1:] for found in batches for entry in found]
        table = np.zeros((axis_size, len(order)), np.int32)
        for p, members in enumerate(ring):
            for c, at in enumerate(members):
                for k, (offset, beside, part) in enumerate(order):
                    its = 1 - c if beside else c
                    source = ring[(p + offset * turn_of[its]) % chips][its]
                    table[at, k] = (source * device_units + part * half) // LANES
        starts = jnp.asarray(table)[me]
        acc, ready, done = [], [], 0
        ends = len(batches) - len(cuts)
        settled = min(5, ends - 1)
        for k, found in enumerate(batches[:ends]):
            coming = batches[k + 1] if k >= settled else []
            at = done + len(found)
            ahead = [(at + j, min(entry[0].shape[1], device_units)) for j, entry in enumerate(coming)]
            out, ready_next = chunk_matmul(
                [entry[0] for entry in found],
                starts,
                done,
                weight,
                acc + ([extra] if k == ends - 1 else []),
                jnp.float32,
                ready,
                ahead,
                k in FAR,
            )
            acc, ready, done = [out], list(ready_next), at
        out = None
        for k, ((row, _), found) in enumerate(zip(cuts, batches[ends:])):
            chunks = [entry[0] for entry in found]
            rest = acc[0]
            if k == len(cuts) - 1:
                rest = rows_matmul(chunks[::2], ready[::2], rest, row, None, False)
                chunks, ready = chunks[1::2], ready[1::2]
            out = rows_matmul(chunks, ready, rest, row, out, True)
        return out

    def local(
        gated_hidden_rows,
        down_base_weight,
        adapter_input_factor,
        adapter_output_weight,
        request_adapter_index,
    ):
        steps, requests, device_units = gated_hidden_rows.shape
        total = steps * requests
        fits = device_units % (2 * LANES) == 0 and total % 384 == 0 and total % (32 * max(long, 1)) == 0
        run = ringed if snake and cores == 2 and long > 1 and fits else plain
        out = run(
            gated_hidden_rows.reshape(total, device_units),
            down_base_weight,
            adapter_input_factor,
            adapter_output_weight,
            request_adapter_index.reshape(total),
        )
        return out.reshape(steps, requests, out.shape[1])

    placed = (
        P(None, "groups", "row"),
        P("row", None),
        P(None, None, "row"),
        P(None, None, "row"),
        P(None, "groups"),
    )


    return jax.shard_map(local, mesh=mesh, in_specs=placed, out_specs=P(None, "groups", "row"), check_vma=False)
```

```python
import jax
import jax.numpy as jnp
import numpy as np
from jax import lax
from jax.experimental import pallas as pl
from jax.experimental.pallas import tpu as pltpu
from jax.sharding import PartitionSpec as P


LANES = 128
FAR = (1, 2, 3, 4)


def chip_ring(mesh):
    line = mesh.devices.reshape(mesh.devices.shape[0], -1)[0]
    chips = {}
    for at, device in enumerate(line):
        place = tuple(getattr(device, "coords", (at, 0, 0)))
        chips.setdefault(place, []).append(at)
    places = list(chips)
    if len({len(c) for c in chips.values()}) != 1:
        return [[at] for at in range(len(line))], False
    used = [k for k in range(len(places[0])) if len({p[k] for p in places}) > 1]
    if len(used) == 2:
        sizes = [len({p[k] for p in places}) for k in used]
        if 2 in sizes and sizes[0] * sizes[1] == len(places):
            short = used[sizes.index(2)]
            long = used[0] if short == used[1] else used[1]
            low = min(p[short] for p in places)
            up = sorted((p for p in places if p[short] == low), key=lambda p: p[long])
            down = sorted((p for p in places if p[short] != low), key=lambda p: -p[long])
            places = up + down
            return [chips[p] for p in places], True
    return [chips[p] for p in places], False


def in_hbm(array):
    return pltpu.with_memory_space_constraint(array, pltpu.HBM)


def cut_block(block, half, near=False):
    def body(x_ref, a_ref, b_ref, sem):
        copies = [
            pltpu.make_async_copy(x_ref.at[:, pl.ds(k * half, half)], out, sem.at[k])
            for k, out in enumerate((a_ref, b_ref))
        ]
        for copy in copies:
            copy.start()
        for copy in copies:
            copy.wait()

    vmem = pl.BlockSpec(memory_space=pltpu.VMEM)
    shape = jax.ShapeDtypeStruct((block.shape[0], half), block.dtype)
    return pl.pallas_call(
        body,
        out_shape=(shape, shape),
        in_specs=[vmem if near else pl.BlockSpec(memory_space=pltpu.HBM)],
        out_specs=(vmem, vmem),
        scratch_shapes=[pltpu.SemaphoreType.DMA((2,))],
        compiler_params=pltpu.CompilerParams(vmem_limit_bytes=4 << 20),
    )(block if near else in_hbm(block))


def project_selected(rows, labels, factors, first):
    count, rank, units = factors.shape
    total = rows[0].shape[0]
    half = units // 2
    wide = count * rank
    part = total // 2

    def body(f_ref, low_ref, high_ref, l_ref, a_any, mine_ref, other_ref, s_ref, a_ref, sem):
        copy = pltpu.make_async_copy(a_any, a_ref, sem)
        copy.start()
        copy.wait()
        full = sum(
            lax.dot_general(
                x_ref[...],
                a_ref[:, k * half : (k + 1) * half],
                (((1,), (1,)), ((), ())),
                preferred_element_type=jnp.float32,
            )
            for k, x_ref in enumerate((low_ref, high_ref))
        )
        own = jnp.zeros((total, rank), jnp.float32)
        for k in range(count):
            own = own + jnp.where(l_ref[...] == k, full[:, k * rank : (k + 1) * rank], 0.0)
        s_ref[...] = jnp.concatenate([own, full[:, :rank]], axis=1)
        at = f_ref[0]
        mine_ref[...] = s_ref[pl.ds(pl.multiple_of(at * part, 8), part), :]
        other_ref[...] = s_ref[pl.ds(pl.multiple_of((1 - at) * part, 8), part), :]

    vmem = pl.BlockSpec(memory_space=pltpu.VMEM)
    anywhere = pl.BlockSpec(memory_space=pltpu.HBM)
    shape = jax.ShapeDtypeStruct((part, 2 * rank), jnp.float32)
    return pl.pallas_call(
        body,
        out_shape=(shape, shape),
        in_specs=[pl.BlockSpec(memory_space=pltpu.SMEM), vmem, vmem, vmem, anywhere],
        out_specs=(vmem, vmem),
        scratch_shapes=[
            pltpu.VMEM((total, 2 * rank), jnp.float32),
            pltpu.VMEM((wide, units), jnp.bfloat16),
            pltpu.SemaphoreType.DMA,
        ],
        cost_estimate=pl.CostEstimate(
            flops=2 * total * wide * units,
            transcendentals=0,
            bytes_accessed=2 * units * (total + wide) + 8 * total * rank,
        ),
        compiler_params=pltpu.CompilerParams(vmem_limit_bytes=12 << 20),
    )(first.reshape(1), *rows, labels[:, None], in_hbm(factors.reshape(wide, units)))


def labels_onehot(adapter_labels, count):
    return adapter_labels[:, None] == jnp.arange(count, dtype=jnp.int32)[None, :]


def select_both(project_rows, adapter_labels, count, rank):
    choose = labels_onehot(adapter_labels, count).astype(jnp.float32)
    total = project_rows.shape[0]
    own = jnp.sum(project_rows.reshape(total, count, rank) * choose[:, :, None], axis=1)
    return jnp.concatenate([own, project_rows[:, :rank]], axis=1)


def expand_factor(shrunk_rows, adapter_labels, adapter_output_weight):
    count, rank, width = adapter_output_weight.shape
    total = shrunk_rows.shape[0]
    choose = labels_onehot(adapter_labels, count).astype(jnp.float32)
    spread = (choose[:, :, None] * shrunk_rows[:, None, :rank].astype(jnp.float32)).reshape(
        total, count * rank
    )
    operand = jnp.concatenate([spread.astype(jnp.bfloat16), shrunk_rows[:, rank:]], axis=1)
    stacked = jnp.concatenate(
        [adapter_output_weight.reshape(count * rank, width), -adapter_output_weight[0]], axis=0
    )
    return jnp.dot(operand, stacked, preferred_element_type=jnp.float32)


def adapter_terms(summed, labels, outputs):
    rank = outputs.shape[1]
    keep = (labels != 0).astype(jnp.float32)[:, None]
    shrunk_rows = (summed * keep).astype(jnp.bfloat16)
    resident = jnp.dot(
        summed[:, rank:], outputs[0].astype(jnp.float32), precision=lax.Precision.HIGHEST
    )
    return resident + expand_factor(shrunk_rows, labels, outputs)


def sum_over_row(summand, axis_size):
    rows, cols = summand.shape
    if rows % axis_size:
        return lax.psum(summand, "row")
    parts = lax.all_to_all(summand, "row", 0, 0, tiled=True)
    mine = jnp.sum(parts.reshape(axis_size, rows // axis_size, cols), axis=0)
    spread = jnp.broadcast_to(mine[None], (axis_size,) + mine.shape).reshape(rows, cols)
    return lax.all_to_all(spread, "row", 0, 0, tiled=True)


def swap(rows, at, pairs):
    part = rows.shape[0] // 2
    low, high = rows[:part], rows[part:]
    got = lax.ppermute(jnp.where(at == 0, high, low), "row", pairs)
    return jnp.where(at == 0, low, high) + got


def join(part, at, pairs):
    got = lax.ppermute(part, "row", pairs)
    return jnp.concatenate([jnp.where(at == 0, part, got), jnp.where(at == 0, got, part)], axis=0)


def rounded_pair(summed):
    rank = summed.shape[1] // 2
    resident = summed[:, rank:]
    left = resident - lax.reduce_precision(resident, exponent_bits=8, mantissa_bits=7)
    return jnp.concatenate([summed[:, :rank], left], axis=1).astype(jnp.bfloat16)


def sum_by_stages(mine, other, side, partner, across, lines):
    got = lax.ppermute(other, "row", partner)
    rows = swap(mine + got, side, across)
    size = len(lines[0])
    piece = rows.shape[0] // size
    parts = lax.all_to_all(rows, "row", 0, 0, axis_index_groups=lines, tiled=True)
    total = rounded_pair(jnp.sum(parts.reshape(size, piece, rows.shape[1]), axis=0))
    spread = jnp.broadcast_to(total[None], (size,) + total.shape).reshape(rows.shape)
    whole = lax.all_to_all(spread, "row", 0, 0, axis_index_groups=lines, tiled=True)
    half = join(whole, side, across)
    return half, lax.ppermute(half, "row", partner)


def chunk_matmul(chunks, starts, first, weight, added, out_dtype, ready, ahead, far=False):
    count = len(chunks)
    rows = chunks[0].shape[0]
    widths = [c.shape[1] for c in chunks]
    features = weight.shape[0]
    later = len(ahead)

    def body(starts_ref, *refs):
        x_refs, refs = refs[:count], refs[count:]
        w_any, refs = refs[0], refs[1:]
        w_refs, refs = refs[: len(ready)], refs[len(ready) :]
        add_refs, refs = refs[: len(added)], refs[len(added) :]
        out_ref, ahead_refs, refs = refs[0], refs[1 : 1 + later], refs[1 + later :]

        def block(at, units):
            start = pl.multiple_of(starts_ref[at] * LANES, LANES)
            return w_any.at[:, pl.ds(start, units)]

        copies = []
        if far:
            near, x_sem, refs = refs[:count], refs[count], refs[count + 1 :]
            arrivals = [pltpu.make_async_copy(x_refs[k], near[k], x_sem.at[k]) for k in range(count)]
            for copy in arrivals:
                copy.start()
            x_refs = near
        if not ready:
            w_refs, w_sem = refs[:count], refs[count]
            for k in range(count):
                copy = pltpu.make_async_copy(block(first + k, widths[k]), w_refs[k], w_sem.at[k])
                copy.start()
                copies.append(copy)
        fetches = [
            pltpu.make_async_copy(block(at, units), ahead_refs[k], refs[-1].at[k])
            for k, (at, units) in enumerate(ahead)
        ]
        for fetch in fetches:
            fetch.start()
        total = None
        for k in range(count):
            if far:
                arrivals[k].wait()
            if copies:
                copies[k].wait()
            part = lax.dot_general(
                x_refs[k][...],
                w_refs[k][...],
                (((1,), (1,)), ((), ())),
                preferred_element_type=jnp.float32,
            )
            total = part if total is None else total + part
        for ref in add_refs:
            total = total + ref[...]
        out_ref[...] = total.astype(out_dtype)
        for fetch in fetches:
            fetch.wait()

    anywhere = pl.BlockSpec(memory_space=pltpu.HBM)
    vmem = pl.BlockSpec(memory_space=pltpu.VMEM)
    scratch = []
    if far:
        chunks = [in_hbm(chunk) for chunk in chunks]
        scratch += [pltpu.VMEM((rows, w), jnp.bfloat16) for w in widths]
        scratch += [pltpu.SemaphoreType.DMA((count,))]
    if not ready:
        scratch += [pltpu.VMEM((features, w), jnp.bfloat16) for w in widths]
        scratch += [pltpu.SemaphoreType.DMA((count,))]
    if later:
        scratch += [pltpu.SemaphoreType.DMA((later,))]
    room = 2 * sum(widths) * (rows + features) + 2 * features * sum(u for _, u in ahead)
    room += 4 * rows * features * (1 + len(added))
    moved = sum(widths) * (rows + features) + features * sum(units for _, units in ahead)
    out = pl.pallas_call(
        body,
        out_shape=[jax.ShapeDtypeStruct((rows, features), out_dtype)]
        + [jax.ShapeDtypeStruct((features, units), jnp.bfloat16) for _, units in ahead],
        in_specs=[pl.BlockSpec(memory_space=pltpu.SMEM)]
        + [anywhere if far else vmem] * count
        + [anywhere]
        + [vmem] * (len(ready) + len(added)),
        out_specs=[vmem] * (1 + later),
        scratch_shapes=scratch,
        cost_estimate=pl.CostEstimate(
            flops=2 * rows * sum(widths) * features,
            transcendentals=0,
            bytes_accessed=2 * moved + 8 * rows * features,
        ),
        compiler_params=pltpu.CompilerParams(vmem_limit_bytes=room + (5 << 20)),
    )(starts, *chunks, in_hbm(weight), *ready, *added)
    return out[0], out[1:]


def row_cuts(total):
    unit = total // 24
    return [(0, 13 * unit), (13 * unit, 11 * unit)]


def rows_matmul(chunks, blocks, acc, row, out, final):
    count = len(chunks)
    rows = chunks[0].shape[0]
    features = blocks[0].shape[0]
    total = acc.shape[0] if out is None else out.shape[0]

    def body(*refs):
        x_refs, w_refs, a_ref, refs = refs[:count], refs[count : 2 * count], refs[2 * count], refs[2 * count + 1 :]
        value = a_ref[...] if a_ref.shape[0] == rows else a_ref[row : row + rows, :]
        for x_ref, w_ref in zip(x_refs, w_refs):
            value = value + lax.dot_general(
                x_ref[...], w_ref[...], (((1,), (1,)), ((), ())), preferred_element_type=jnp.float32
            )
        if final:
            o_ref, s_ref, sem = refs[-3:]
            s_ref[...] = value.astype(jnp.bfloat16)
            copy = pltpu.make_async_copy(s_ref, o_ref.at[pl.ds(row, rows)], sem)
            copy.start()
            copy.wait()
        else:
            refs[0][...] = value

    anywhere = pl.BlockSpec(memory_space=pltpu.HBM)
    vmem = pl.BlockSpec(memory_space=pltpu.VMEM)
    shape = jax.ShapeDtypeStruct((total, features), jnp.bfloat16)
    if not final:
        shape = jax.ShapeDtypeStruct((rows, features), jnp.float32)
    return pl.pallas_call(
        body,
        out_shape=shape,
        in_specs=[vmem] * (2 * count + 1) + ([] if out is None else [anywhere]),
        out_specs=anywhere if final else vmem,
        scratch_shapes=[pltpu.VMEM((rows, features), jnp.bfloat16), pltpu.SemaphoreType.DMA] if final else [],
        input_output_aliases={} if out is None else {2 * count + 1: 0},
        compiler_params=pltpu.CompilerParams(vmem_limit_bytes=16 << 20),
    )(*chunks, *blocks, acc, *([] if out is None else [out]))


def adapter_kernel(mine, other, core, labels, outputs):
    count, rank, width = outputs.shape
    part, cols = mine.shape
    total = 2 * part

    def body(core_ref, mine_ref, other_ref, l_ref, w_ref, o_ref, s_ref):
        at = core_ref[0]
        s_ref[pl.ds(pl.multiple_of(at * part, 16), part), :] = mine_ref[...]
        s_ref[pl.ds(pl.multiple_of((1 - at) * part, 16), part), :] = other_ref[...]
        pair = s_ref[...]
        label = l_ref[...]
        own = pair[:, :rank].astype(jnp.float32)
        spread = jnp.concatenate([jnp.where(label == k, own, 0.0) for k in range(count)], axis=1)
        update = jnp.dot(
            spread.astype(jnp.bfloat16), w_ref[...], preferred_element_type=jnp.float32
        )
        o_ref[...] = update + jnp.dot(
            pair[:, rank:], w_ref[:rank, :], preferred_element_type=jnp.float32
        )

    vmem = pl.BlockSpec(memory_space=pltpu.VMEM)
    return pl.pallas_call(
        body,
        out_shape=jax.ShapeDtypeStruct((total, width), jnp.float32),
        in_specs=[pl.BlockSpec(memory_space=pltpu.SMEM)] + [vmem] * 4,
        out_specs=vmem,
        scratch_shapes=[pltpu.VMEM((total, cols), jnp.bfloat16)],
        cost_estimate=pl.CostEstimate(
            flops=2 * total * (count + 1) * rank * width,
            transcendentals=0,
            bytes_accessed=2 * count * rank * width + 2 * total * cols + 4 * total * width,
        ),
        compiler_params=pltpu.CompilerParams(vmem_limit_bytes=12 << 20),
    )(core.reshape(1), mine, other, labels[:, None], outputs.reshape(count * rank, width))


def solution(mesh):
    axis_size = mesh.shape["row"]
    ring, snake = chip_ring(mesh)
    chips, cores = len(ring), len(ring[0])
    turn_of = [1, -1]
    forward = [
        (ring[p][c], ring[(p + turn_of[c % 2]) % chips][c]) for p in range(chips) for c in range(cores)
    ]
    backward = [(b, a) for a, b in forward]
    partner = [(members[c], members[1 - c]) for members in ring for c in range(cores)] if cores == 2 else []

    long = chips // 2
    across = [(ring[p][c], ring[chips - 1 - p][c]) for p in range(chips) for c in range(cores)]
    lines = [
        [ring[p][c] for p in range(lo, lo + long)] for lo in (0, long) for c in range(cores)
    ]
    place = np.zeros((axis_size, 2), np.int32)
    for p, members in enumerate(ring):
        for c, at in enumerate(members):
            place[at] = c, int(p >= long)

    def plain(flat, weight, factors, outputs, labels):
        count, rank, units = factors.shape
        project_rows = jnp.dot(
            flat, factors.reshape(count * rank, units).T, preferred_element_type=jnp.float32
        )
        summed = sum_over_row(select_both(project_rows, labels, count, rank), axis_size)
        base = lax.dot_general(
            lax.all_gather(flat, "row", axis=1, tiled=True),
            weight,
            (((1,), (1,)), ((), ())),
            preferred_element_type=jnp.float32,
        )
        return (base + adapter_terms(summed, labels, outputs)).astype(jnp.bfloat16)

    def ringed(flat, weight, factors, outputs, labels):
        device_units = flat.shape[1]
        half = device_units // 2
        total = flat.shape[0]
        cuts = row_cuts(total)
        me = lax.axis_index("row")
        core, side = [jnp.asarray(place)[me][k] for k in range(2)]
        own = cut_block(flat, half)
        mine, other = project_selected(own, labels, factors, core)
        halves = sum_by_stages(mine, other, side, partner, across, lines)
        extra = adapter_kernel(*halves, core, labels, outputs)

        beside = lax.ppermute(flat, "row", partner)
        batches = [[(own[part], 0, False, part) for part in range(2)] + [(beside, 0, True, 0)]]

        def hop(data, pairs, offset, part):
            data = lax.ppermute(data, "row", pairs)
            beside = lax.ppermute(data, "row", partner)
            return data, [(data, offset, False, part), (beside, offset, True, part)]

        block, whole = hop(flat, forward, -1, 0)
        ups = list(cut_block(block, half, True))
        downs = list(own)
        for s in range(2 * long - 2):
            distance, turn = s // 2 + 1, s % 2
            downs[1 - turn], found = hop(downs[1 - turn], backward, distance, 1 - turn)
            if s == 1:
                found = whole + found
            elif s > 1:
                ups[turn], more = hop(ups[turn], forward, -distance, turn)
                found = more + found
            batches.append(found)
        for row, rows in cuts:
            _, found = hop(ups[0][row : row + rows], forward, -long, 0)
            batches.append(found + hop(downs[1][row : row + rows], backward, long, 1)[1])
        order = [entry[1:] for found in batches for entry in found]
        table = np.zeros((axis_size, len(order)), np.int32)
        for p, members in enumerate(ring):
            for c, at in enumerate(members):
                for k, (offset, beside, part) in enumerate(order):
                    its = 1 - c if beside else c
                    source = ring[(p + offset * turn_of[its]) % chips][its]
                    table[at, k] = (source * device_units + part * half) // LANES
        starts = jnp.asarray(table)[me]
        acc, ready, done = [], [], 0
        ends = len(batches) - len(cuts)
        settled = min(5, ends - 1)
        for k, found in enumerate(batches[:ends]):
            coming = batches[k + 1] if k >= settled else []
            at = done + len(found)
            ahead = [(at + j, min(entry[0].shape[1], device_units)) for j, entry in enumerate(coming)]
            out, ready_next = chunk_matmul(
                [entry[0] for entry in found],
                starts,
                done,
                weight,
                acc + ([extra] if k == ends - 1 else []),
                jnp.float32,
                ready,
                ahead,
                k in FAR,
            )
            acc, ready, done = [out], list(ready_next), at
        out = None
        for k, ((row, _), found) in enumerate(zip(cuts, batches[ends:])):
            chunks = [entry[0] for entry in found]
            rest = acc[0]
            if k == len(cuts) - 1:
                rest = rows_matmul(chunks[::2], ready[::2], rest, row, None, False)
                chunks, ready = chunks[1::2], ready[1::2]
            out = rows_matmul(chunks, ready, rest, row, out, True)
        return out

    def local(
        gated_hidden_rows,
        down_base_weight,
        adapter_input_factor,
        adapter_output_weight,
        request_adapter_index,
    ):
        steps, requests, device_units = gated_hidden_rows.shape
        total = steps * requests
        fits = device_units % (2 * LANES) == 0 and total % 384 == 0 and total % (32 * max(long, 1)) == 0
        run = ringed if snake and cores == 2 and long > 1 and fits else plain
        out = run(
            gated_hidden_rows.reshape(total, device_units),
            down_base_weight,
            adapter_input_factor,
            adapter_output_weight,
            request_adapter_index.reshape(total),
        )
        return out.reshape(steps, requests, out.shape[1])

    placed = (
        P(None, "groups", "row"),
        P("row", None),
        P(None, None, "row"),
        P(None, None, "row"),
        P(None, "groups"),
    )


    return jax.shard_map(local, mesh=mesh, in_specs=placed, out_specs=P(None, "groups", "row"), check_vma=False)
```
